32 devices in a mesh: rep: 4 (over z), fsdp: 8 (over y, x, core).
Axes of the slice: x: 2, y: 2, z: 4, core: 2. Of those that a mesh axis runs over, the one named last changes fastest.
Arguments:
- tokens: bfloat16 [12, 1024, 2048], P('rep', 'fsdp'), may hold values from -6 to 6
- layer_input: bfloat16 [12, 1024, 256], P('rep', 'fsdp'), may hold values from -6 to 6
- cotangent: bfloat16 [12, 1024, 2048], P('rep', 'fsdp'), may hold values from -6 to 6
- lengths: int32 [12], replicated, may hold values from 256 to 1024, as said below
- deal_order: int32 [12], replicated, may hold values from 0 to 11, as said below
- attention_input_weight: bfloat16 [2048, 3072], P('fsdp'), may hold values from -0.125 to 0.125
- attn_out: bfloat16 [2048, 2048], P('fsdp'), may hold values from -0.125 to 0.125
- gate_up: bfloat16 [2048, 16384], P('fsdp'), may hold values from -0.125 to 0.125
- ffn_down: bfloat16 [2048, 8192], P('fsdp'), may hold values from -0.0625 to 0.0625
- laurel_pair: bfloat16 [2048, 128], P('fsdp'), may hold values from -0.125 to 0.125
- layer_pair: bfloat16 [2048, 512], P('fsdp'), may hold values from -0.125 to 0.125
- norm_gains: bfloat16 [6, 2048], P(None, 'fsdp'), may hold values from 0.5 to 1.5
- head_gains: bfloat16 [2, 256], replicated, may hold values from 0.5 to 1.5
Outputs:
- mixed: bfloat16 [12, 1024, 2048], P('rep', 'fsdp')
- input_grad: bfloat16 [12, 1024, 2048], P('rep', 'fsdp')
- layer_input_grad: bfloat16 [12, 1024, 256], P('rep', 'fsdp')
- attn_in_grad: float32 [2048, 3072], P('fsdp')
- attn_out_grad: float32 [2048, 2048], P('fsdp')
- gate_up_grad: float32 [2048, 16384], P('fsdp')
- ffn_down_grad: float32 [2048, 8192], P('fsdp')
- laurel_pair_grad: float32 [2048, 128], P('fsdp')
- layer_pair_grad: float32 [2048, 512], P('fsdp')
- norm_gains_grad: float32 [6, 2048], P(None, 'fsdp')
- head_gains_grad: float32 [2, 256], replicated
The draws below stay inside these ranges and needn't reach their ends.
Inputs may be any that keep to these rules, and one draw needn't show every extreme that they name: `lengths`: in every draw one sequence has length 1024 and one has 256. `deal_order`: A permutation of the 12 sequences. Slots g * 3 to g * 3 + 2 form group g, and the sequences of one group come from 3 different blocks of 3 given sequences (block r holds given sequences r * 3 to r * 3 + 2).
All inputs are finite; a program needn't handle non-finite values.
Results may differ from the reference program's by a relative error of at most 0.023.
Values may be sent and summed in bfloat16 or wider, within the bound.
No kernel may reach another device: no remote copies, remote signals or barrier semaphores. Data moves between devices by JAX's collectives and lax.ppermute only.
A program may use at most 448 MiB of HBM per device.

```python
import jax
import jax.numpy as jnp
from jax import lax

MODEL_DIM = 2048
QUERY_HEADS = 8
KEY_VALUE_HEADS = 2
HEAD_DIM = 256
HIDDEN_UNITS = 8192
RESIDUAL_RANK = 64
PER_LAYER_WIDTH = 256
WINDOW = 512
SLOT_POSITIONS = 1024
GROUP_SEQUENCES = 3
NSEQ = 12


def draw_lengths(key, part):
    values = jax.random.randint(jax.random.fold_in(key, 11), (NSEQ,), SLOT_POSITIONS // 4, SLOT_POSITIONS + 1)
    picks = jax.random.permutation(jax.random.fold_in(key, 12), NSEQ)
    values = values.at[picks[0]].set(SLOT_POSITIONS)
    values = values.at[picks[1]].set(SLOT_POSITIONS // 4)
    return values.astype(jnp.int32)


def draw_deal_order(key, part):
    groups = NSEQ // GROUP_SEQUENCES
    labels = jax.random.permutation(jax.random.fold_in(key, 21), groups).astype(jnp.int32)
    inverse = jnp.zeros((groups,), jnp.int32).at[labels].set(jnp.arange(groups, dtype=jnp.int32))
    shifts = jax.random.permutation(jax.random.fold_in(key, 22), groups)[:GROUP_SEQUENCES].astype(jnp.int32)
    subkeys = jax.random.split(jax.random.fold_in(key, 23), groups)
    doc_orders = jax.vmap(lambda sub_key: jax.random.permutation(sub_key, GROUP_SEQUENCES))(subkeys).astype(jnp.int32)
    targets = jnp.arange(groups, dtype=jnp.int32)[:, None]
    slot_k = jnp.arange(GROUP_SEQUENCES, dtype=jnp.int32)[None, :]
    source = labels[(inverse[targets] + shifts[slot_k]) % groups]
    chosen = doc_orders[source, slot_k]
    return (source * GROUP_SEQUENCES + chosen).reshape(-1).astype(jnp.int32)


def steps_of(rng, extent, cuts, smallest, largest):
    factor_of, own = 1.0, jax.random.fold_in(rng, 6)
    for dim, blocks in cuts:
        steps = jnp.exp(jax.random.uniform(jax.random.fold_in(own, dim), (blocks,), jnp.float32, smallest / len(cuts), largest / len(cuts)))
        factor_of = factor_of * jnp.repeat(steps, extent[dim] // blocks).reshape([-1 if axis == dim else 1 for axis in range(len(extent))])
    return factor_of


def scatter_about(stream_key, extent, width, limit, shards=(), kind=jnp.bfloat16):
    gain = steps_of(stream_key, extent, shards, -0.22, 0.18) if shards else 1.0
    entries = jax.random.normal(stream_key, extent, jnp.float32) * width * gain
    return jnp.minimum(jnp.maximum(entries, -limit), limit).astype(kind)


def setup_inputs(seed: int = 0) -> dict:
    streams_of = jax.random.split(jax.random.key(seed), 14)
    tokens = scatter_about(streams_of[0], (NSEQ, SLOT_POSITIONS, MODEL_DIM), 1.0, 6.0, ((0, 4), (1, 8)))
    layer_input = scatter_about(streams_of[1], (NSEQ, SLOT_POSITIONS, PER_LAYER_WIDTH), 1.0, 6.0, ((0, 4), (1, 8)))
    cotangent = scatter_about(streams_of[2], (NSEQ, SLOT_POSITIONS, MODEL_DIM), 1.0, 6.0, ((0, 4), (1, 8)))
    lengths = draw_lengths(jax.random.fold_in(streams_of[13], 71), 0)
    deal_order = draw_deal_order(jax.random.fold_in(streams_of[13], 71), 0)
    attention_input_weight = scatter_about(streams_of[5], (MODEL_DIM, (QUERY_HEADS + 2 * KEY_VALUE_HEADS) * HEAD_DIM), MODEL_DIM ** -0.5, 0.125, ((0, 8),))
    attn_out = scatter_about(streams_of[6], (MODEL_DIM, QUERY_HEADS * HEAD_DIM), (QUERY_HEADS * HEAD_DIM) ** -0.5, 0.125, ((0, 8),))
    gate_up = scatter_about(streams_of[7], (MODEL_DIM, 2 * HIDDEN_UNITS), MODEL_DIM ** -0.5, 0.125, ((0, 8),))
    ffn_down = scatter_about(streams_of[8], (MODEL_DIM, HIDDEN_UNITS), HIDDEN_UNITS ** -0.5, 0.0625, ((0, 8),))
    laurel_pair = scatter_about(streams_of[9], (MODEL_DIM, 2 * RESIDUAL_RANK), MODEL_DIM ** -0.5, 0.125, ((0, 8),))
    layer_pair = scatter_about(streams_of[10], (MODEL_DIM, 2 * PER_LAYER_WIDTH), MODEL_DIM ** -0.5, 0.125, ((0, 8),))
    norm_gains = jnp.clip(1.0 + 0.1 * jax.random.normal(streams_of[11], (6, MODEL_DIM), jnp.float32), 0.5, 1.5).astype(jnp.bfloat16)
    head_gains = jnp.clip(1.0 + 0.1 * jax.random.normal(streams_of[12], (2, HEAD_DIM), jnp.float32), 0.5, 1.5).astype(jnp.bfloat16)
    return dict(tokens=tokens, layer_input=layer_input, cotangent=cotangent, lengths=lengths, deal_order=deal_order, attention_input_weight=attention_input_weight, attn_out=attn_out, gate_up=gate_up, ffn_down=ffn_down, laurel_pair=laurel_pair, layer_pair=layer_pair, norm_gains=norm_gains, head_gains=head_gains)


@jax.custom_vjp
def residual_lowrank(v):
    return lax.optimization_barrier(v.astype(jnp.bfloat16)).astype(jnp.float32)

@jax.custom_vjp
def low_back(v):
    return v

def low_keep(v):
    return (residual_lowrank(v), None)

def low_pass(kept, grad):
    return (grad,)

def back_keep(v):
    return (v, None)

def back_low(kept, grad):
    return (residual_lowrank(grad),)
residual_lowrank.defvjp(low_keep, low_pass)
low_back.defvjp(back_keep, back_low)
EPS = 1e-06
BASE = 10000.0
ROOT_HALF = 0.7071067811865476
NEG_FILL = -1e+30
HIGHEST = lax.Precision.HIGHEST

def product(left, right):
    return jnp.dot(left, right, precision=HIGHEST)

def rms_norm(values, scales):
    return values * lax.rsqrt(lax.optimization_barrier(jnp.mean(values * values, axis=-1, keepdims=True)) + EPS) * scales

def gelu_tanh(values):
    return jax.nn.gelu(values, approximate=True)

def frequencies():
    return 1.0 / BASE ** (jnp.arange(HEAD_DIM // 2, dtype=jnp.float32) * 2.0 / HEAD_DIM)

def rotary(values, angles):
    middle = values.shape[-1] // 2
    lower_part = values[..., :middle]
    upper_part = values[..., middle:]
    cosine = jnp.cos(angles)
    sine_part = jnp.sin(angles)
    return jnp.concatenate([lower_part * cosine - upper_part * sine_part, upper_part * cosine + lower_part * sine_part], axis=-1)

def qkv_post(query_key_value, head_scales, angles):
    count_of_rows = query_key_value.shape[0]
    query_single = query_key_value[:, :QUERY_HEADS * HEAD_DIM].reshape(count_of_rows, QUERY_HEADS, HEAD_DIM)
    keyed_rows = query_key_value[:, QUERY_HEADS * HEAD_DIM:(QUERY_HEADS + KEY_VALUE_HEADS) * HEAD_DIM].reshape(count_of_rows, KEY_VALUE_HEADS, HEAD_DIM)
    valued_rows = query_key_value[:, (QUERY_HEADS + KEY_VALUE_HEADS) * HEAD_DIM:].reshape(count_of_rows, KEY_VALUE_HEADS, HEAD_DIM)
    query_single = rotary(rms_norm(query_single, head_scales[0]), angles[:, None, :])
    keyed_rows = rotary(rms_norm(keyed_rows, head_scales[1]), angles[:, None, :])
    valued_rows = rms_norm(valued_rows, 1.0)
    return (query_single.reshape(count_of_rows, QUERY_HEADS * HEAD_DIM), keyed_rows.reshape(count_of_rows, KEY_VALUE_HEADS * HEAD_DIM), valued_rows.reshape(count_of_rows, KEY_VALUE_HEADS * HEAD_DIM))

def group_layer(items, params):
    group_x, group_layer_in, slot_lens, slot_offsets = items
    attention_input_weight, attn_out, gate_up, ffn_down, laurel_pair, layer_pair, norm_gains, head_gains = params
    rows = group_x.reshape(GROUP_SEQUENCES * SLOT_POSITIONS, MODEL_DIM)
    layer_rows = group_layer_in.reshape(GROUP_SEQUENCES * SLOT_POSITIONS, PER_LAYER_WIDTH)
    positions = slot_offsets[:, None] + jnp.arange(SLOT_POSITIONS, dtype=jnp.int32)[None, :]
    angles = positions.reshape(-1).astype(jnp.float32)[:, None] * frequencies()[None, :]
    hidden = rms_norm(rows, norm_gains[0])
    hidden_b = residual_lowrank(hidden)
    query_key_value = low_back(product(hidden_b, attention_input_weight))
    query_single, keyed_rows, valued_rows = qkv_post(query_key_value, head_gains, angles)
    query_single = residual_lowrank(query_single).reshape(GROUP_SEQUENCES, SLOT_POSITIONS, KEY_VALUE_HEADS, QUERY_HEADS // KEY_VALUE_HEADS, HEAD_DIM)
    keyed_rows = residual_lowrank(keyed_rows).reshape(GROUP_SEQUENCES * SLOT_POSITIONS, KEY_VALUE_HEADS, HEAD_DIM)
    valued_rows = residual_lowrank(valued_rows).reshape(GROUP_SEQUENCES * SLOT_POSITIONS, KEY_VALUE_HEADS, HEAD_DIM)
    key_index = jnp.arange(GROUP_SEQUENCES * SLOT_POSITIONS, dtype=jnp.int32)
    key_slot = key_index // SLOT_POSITIONS
    key_pos = key_index % SLOT_POSITIONS
    key_stream = positions.reshape(-1)
    key_valid = key_pos < slot_lens[key_slot]
    query_pos = jnp.arange(SLOT_POSITIONS, dtype=jnp.int32)

    def attend(index_of_slot):
        query_rows = query_single[index_of_slot]
        scores = low_back(jnp.einsum('pagh,jah->agpj', query_rows, keyed_rows, precision=HIGHEST) * HEAD_DIM ** (-0.5))
        stream_here = positions[index_of_slot]
        reach = key_valid[None, :] & (key_stream[None, :] <= stream_here[:, None]) & (stream_here[:, None] - key_stream[None, :] < WINDOW)
        diagonal = (key_slot[None, :] == index_of_slot) & (key_pos[None, :] == query_pos[:, None])
        masked = jnp.where((reach | diagonal)[None, None], scores, NEG_FILL)
        top = lax.optimization_barrier(jnp.max(masked, axis=-1, keepdims=True))
        expd = jnp.exp(masked - top)
        probs = residual_lowrank(expd / lax.optimization_barrier(jnp.sum(expd, axis=-1, keepdims=True)))
        return jnp.einsum('agpj,jah->pagh', probs, valued_rows, precision=HIGHEST).reshape(SLOT_POSITIONS, QUERY_HEADS * HEAD_DIM)
    attended = lax.map(jax.checkpoint(attend), jnp.arange(GROUP_SEQUENCES, dtype=jnp.int32))
    attended_b = low_back(residual_lowrank(attended.reshape(GROUP_SEQUENCES * SLOT_POSITIONS, QUERY_HEADS * HEAD_DIM)))
    attn_proj = low_back(product(attended_b, attn_out.T))
    laurel_mid = residual_lowrank(low_back(product(hidden_b, laurel_pair[:, :RESIDUAL_RANK])))
    laurel_back = low_back(product(laurel_mid, laurel_pair[:, RESIDUAL_RANK:].T))
    first_sum = (rows + rms_norm(attn_proj, norm_gains[2]) + hidden + rms_norm(laurel_back, norm_gains[1])) * ROOT_HALF
    ffn_in = residual_lowrank(rms_norm(first_sum, norm_gains[3]))
    gate_vals = low_back(product(ffn_in, gate_up))
    act_b = residual_lowrank(low_back(gelu_tanh(gate_vals[:, :HIDDEN_UNITS]) * gate_vals[:, HIDDEN_UNITS:]))
    down_vals = low_back(product(act_b, ffn_down.T))
    second_sum = first_sum + rms_norm(down_vals, norm_gains[4])
    second_b = residual_lowrank(second_sum)
    layer_gate = low_back(product(second_b, layer_pair[:, :PER_LAYER_WIDTH]))
    layer_mix = residual_lowrank(low_back(gelu_tanh(layer_gate) * layer_rows))
    layer_back = low_back(product(layer_mix, layer_pair[:, PER_LAYER_WIDTH:].T))
    output = second_sum + rms_norm(layer_back, norm_gains[5])
    return output.reshape(GROUP_SEQUENCES, SLOT_POSITIONS, MODEL_DIM)

def reference(tokens, layer_input, cotangent, lengths, deal_order, attention_input_weight, attn_out, gate_up, ffn_down, laurel_pair, layer_pair, norm_gains, head_gains):
    groups = NSEQ // GROUP_SEQUENCES
    order_groups = deal_order.reshape(groups, GROUP_SEQUENCES)
    group_lens = lengths[order_groups]
    group_offsets = jnp.cumsum(group_lens, axis=1) - group_lens
    live = (jnp.arange(SLOT_POSITIONS, dtype=jnp.int32)[None, :] < lengths[:, None]).astype(jnp.float32)[:, :, None]

    def forward(x_all, layer_all, params):
        group_x = x_all[order_groups]
        group_layer_in = layer_all[order_groups]
        outputs = lax.map(jax.checkpoint(lambda items: group_layer(items, params)), (group_x, group_layer_in, group_lens, group_offsets))
        placed = jnp.zeros((NSEQ, SLOT_POSITIONS, MODEL_DIM), jnp.float32).at[deal_order].set(outputs.reshape(NSEQ, SLOT_POSITIONS, MODEL_DIM))
        return placed * live
    params = (attention_input_weight.astype(jnp.float32), attn_out.astype(jnp.float32), gate_up.astype(jnp.float32), ffn_down.astype(jnp.float32), laurel_pair.astype(jnp.float32), layer_pair.astype(jnp.float32), norm_gains.astype(jnp.float32), head_gains.astype(jnp.float32))
    mixed, pullback = jax.vjp(forward, tokens.astype(jnp.float32), layer_input.astype(jnp.float32), params)
    grad_x, grad_layer, grad_params = pullback(cotangent.astype(jnp.float32))
    return (mixed.astype(jnp.bfloat16), grad_x.astype(jnp.bfloat16), grad_layer.astype(jnp.bfloat16), grad_params[0], grad_params[1], grad_params[2], grad_params[3], grad_params[4], grad_params[5], grad_params[6], grad_params[7])
```

```python
import jax
import jax.numpy as jnp
import numpy as np
from jax import lax
from jax.experimental import pallas as pl
from jax.experimental.pallas import tpu as pltpu
from jax.sharding import PartitionSpec as P

QUERY_HEADS = 8
KEY_VALUE_HEADS = 2
HEADS_PER_KEY = QUERY_HEADS // KEY_VALUE_HEADS
HEAD_DIM = 256
HALF_DIM = HEAD_DIM // 2
HIDDEN_UNITS = 8192
RESIDUAL_RANK = 64
PER_LAYER_WIDTH = 256
WINDOW = 512
QUERY_WIDTH = QUERY_HEADS * HEAD_DIM
KEY_WIDTH = KEY_VALUE_HEADS * HEAD_DIM

EPS = 1e-06
BASE = 10000.0
ROOT_HALF = 0.7071067811865476
NEG_FILL = -1e30
SCALE = HEAD_DIM ** (-0.5)

F32 = jnp.float32
BF16 = jnp.bfloat16


def rms_norm(values, scales):
    return values * lax.rsqrt(jnp.mean(values * values, axis=-1, keepdims=True) + EPS) * scales


def gelu_tanh(values):
    return jax.nn.gelu(values, approximate=True)


def frequencies():
    return 1.0 / BASE ** (jnp.arange(HALF_DIM, dtype=F32) * 2.0 / HEAD_DIM)


def combine(x_float, attn_proj, laurel_back, hidden, scale_one, scale_two):
    return (
        x_float + rms_norm(attn_proj, scale_two) + hidden + rms_norm(laurel_back, scale_one)
    ) * ROOT_HALF


def gated(gate, up):
    return gelu_tanh(gate) * up


def residual_norm(base, values, scales):
    return base + rms_norm(values, scales)


def to_low(values):
    return values.astype(BF16)


def dot(left, right):
    return jnp.dot(left, right, preferred_element_type=F32)


def dot_t(left, right):
    return lax.dot_general(left, right, (((1,), (1,)), ((), ())), preferred_element_type=F32)


def t_dot(left, right):
    return lax.dot_general(left, right, (((0,), (0,)), ((), ())), preferred_element_type=F32)


def fsdp_phases(count):
    bits = [1 << k for k in range(1, count.bit_length() - 1)]
    phases = []
    for k in range(len(bits)):
        phases.append([i ^ (bits[k] if i % 2 == 0 else bits[len(bits) - 1 - k]) for i in range(count)])
    phases.append([i ^ 1 for i in range(count)])
    return phases


def rep_phases(count):
    bits = [1 << k for k in range(count.bit_length() - 1)]
    return [[i ^ b for i in range(count)] for b in reversed(bits)]


def slot_table(phases, count):
    held = [[i] for i in range(count)]
    for perm in phases:
        held = [held[i] + held[perm[i]] for i in range(count)]
    return np.array(held, dtype=np.int32).T


class Exchange:
    def __init__(self, axis, phases, count):
        self.axis = axis
        self.count = count
        self.perms = [[(i, p[i]) for i in range(count)] for p in phases]
        self.table = slot_table(phases, count)
        inverse = np.zeros_like(self.table)
        for i in range(count):
            inverse[self.table[:, i], i] = np.arange(count)
        self.inverse = inverse

    def sources(self, index):
        return lax.dynamic_index_in_dim(jnp.asarray(self.table), index, 1, keepdims=False)

    def slots(self, index):
        return lax.dynamic_index_in_dim(jnp.asarray(self.inverse), index, 1, keepdims=False)

    def gather(self, piece):
        for perm in self.perms:
            piece = jnp.concatenate([piece, lax.ppermute(piece, self.axis, perm)], axis=0)
        return piece

    def scatter(self, parts):
        for perm in reversed(self.perms):
            middle = parts.shape[0] // 2
            got = lax.ppermute(parts[middle:], self.axis, perm)
            parts = (parts[:middle].astype(F32) + got.astype(F32)).astype(parts.dtype)
        return parts

    def total(self, value):
        for perm in self.perms:
            value = value + lax.ppermute(value, self.axis, perm)
        return value


def heads_fwd_body(qkv_ref, cos_ref, sin_ref, gains_ref, q_ref, kv_ref):
    cosine = cos_ref[...]
    sine = sin_ref[...]
    for c in range(QUERY_HEADS + 2 * KEY_VALUE_HEADS):
        head = qkv_ref[:, c * HEAD_DIM : (c + 1) * HEAD_DIM]
        normed = head * lax.rsqrt(jnp.mean(head * head, axis=-1, keepdims=True) + EPS)
        if c < QUERY_HEADS + KEY_VALUE_HEADS:
            row = 0 if c < QUERY_HEADS else 1
            normed = normed * gains_ref[row : row + 1, :]
            low = normed[:, :HALF_DIM]
            high = normed[:, HALF_DIM:]
            first = to_low(low * cosine - high * sine)
            second = to_low(high * cosine + low * sine)
        else:
            first = to_low(normed[:, :HALF_DIM])
            second = to_low(normed[:, HALF_DIM:])
        if c < QUERY_HEADS:
            q_ref[:, c * HEAD_DIM : c * HEAD_DIM + HALF_DIM] = first
            q_ref[:, c * HEAD_DIM + HALF_DIM : (c + 1) * HEAD_DIM] = second
        else:
            at = (c - QUERY_HEADS) * HEAD_DIM
            kv_ref[:, at : at + HALF_DIM] = first
            kv_ref[:, at + HALF_DIM : at + HEAD_DIM] = second


def heads_fwd(qkv, cosine, sine, head_scales, block):
    rows, width = qkv.shape
    return pl.pallas_call(
        heads_fwd_body,
        grid=(rows // block,),
        in_specs=[
            pl.BlockSpec((block, width), lambda i: (i, 0)),
            pl.BlockSpec((block, HALF_DIM), lambda i: (i, 0)),
            pl.BlockSpec((block, HALF_DIM), lambda i: (i, 0)),
            pl.BlockSpec((2, HEAD_DIM), lambda i: (0, 0)),
        ],
        out_specs=[
            pl.BlockSpec((block, QUERY_WIDTH), lambda i: (i, 0)),
            pl.BlockSpec((block, 2 * KEY_WIDTH), lambda i: (i, 0)),
        ],
        out_shape=[
            jax.ShapeDtypeStruct((rows, QUERY_WIDTH), BF16),
            jax.ShapeDtypeStruct((rows, 2 * KEY_WIDTH), BF16),
        ],
        name="heads_fwd",
    )(qkv, cosine, sine, head_scales)


def heads_bwd_body(qkv_ref, cos_ref, sin_ref, gains_ref, gq_ref, gkv_ref, out_ref, gain_ref):
    @pl.when(pl.program_id(0) == 0)
    def _():
        gain_ref[...] = jnp.zeros_like(gain_ref)

    cosine = cos_ref[...]
    sine = sin_ref[...]
    sums = [jnp.zeros((1, HEAD_DIM), F32), jnp.zeros((1, HEAD_DIM), F32)]
    for c in range(QUERY_HEADS + 2 * KEY_VALUE_HEADS):
        head = qkv_ref[:, c * HEAD_DIM : (c + 1) * HEAD_DIM]
        scale = lax.rsqrt(jnp.mean(head * head, axis=-1, keepdims=True) + EPS)
        normed = head * scale
        if c < QUERY_HEADS:
            grad = gq_ref[:, c * HEAD_DIM : (c + 1) * HEAD_DIM].astype(F32)
        else:
            at = (c - QUERY_HEADS) * HEAD_DIM
            grad = gkv_ref[:, at : at + HEAD_DIM].astype(F32)
        if c < QUERY_HEADS + KEY_VALUE_HEADS:
            row = 0 if c < QUERY_HEADS else 1
            first = grad[:, :HALF_DIM]
            second = grad[:, HALF_DIM:]
            grad = jnp.concatenate(
                [first * cosine + second * sine, second * cosine - first * sine], axis=1
            )
            sums[row] = sums[row] + jnp.sum(grad * normed, axis=0, keepdims=True)
            grad = grad * gains_ref[row : row + 1, :]
        back = scale * (grad - normed * jnp.mean(grad * normed, axis=-1, keepdims=True))
        out_ref[:, c * HEAD_DIM : (c + 1) * HEAD_DIM] = to_low(back)
    gain_ref[...] += jnp.concatenate(sums, axis=0)


def heads_bwd(qkv, cosine, sine, head_scales, grad_query, grad_kv, block):
    rows, width = qkv.shape
    return pl.pallas_call(
        heads_bwd_body,
        grid=(rows // block,),
        in_specs=[
            pl.BlockSpec((block, width), lambda i: (i, 0)),
            pl.BlockSpec((block, HALF_DIM), lambda i: (i, 0)),
            pl.BlockSpec((block, HALF_DIM), lambda i: (i, 0)),
            pl.BlockSpec((2, HEAD_DIM), lambda i: (0, 0)),
            pl.BlockSpec((block, QUERY_WIDTH), lambda i: (i, 0)),
            pl.BlockSpec((block, 2 * KEY_WIDTH), lambda i: (i, 0)),
        ],
        out_specs=[
            pl.BlockSpec((block, width), lambda i: (i, 0)),
            pl.BlockSpec((2, HEAD_DIM), lambda i: (0, 0)),
        ],
        out_shape=[
            jax.ShapeDtypeStruct((rows, width), BF16),
            jax.ShapeDtypeStruct((2, HEAD_DIM), F32),
        ],
        name="heads_bwd",
    )(qkv, cosine, sine, head_scales, grad_query, grad_kv)


def load_window(meta_ref, kv_ref, pw_ref, keys_ref, sequences, positions, window_rows, shards):
    blocks = WINDOW // positions + 1
    per_block = positions // window_rows
    for b in range(blocks):
        slot = meta_ref[sequences + b]

        @pl.when(slot >= 0)
        def _():
            keys_ref[b * positions : (b + 1) * positions, :] = kv_ref[jnp.maximum(slot, 0), 0]

        @pl.when(slot < 0)
        def _():
            for m in range(per_block):
                piece = meta_ref[sequences + blocks + b * per_block + m]
                at = b * positions + m * window_rows
                keys_ref[at : at + window_rows, :] = pw_ref[piece, 0]


def window_mask(meta_ref, positions):
    width = WINDOW + positions
    row = lax.broadcasted_iota(jnp.int32, (positions, width), 0)
    col = lax.broadcasted_iota(jnp.int32, (positions, width), 1)
    low = meta_ref[pl.program_id(0)]
    return (col > row) & (col <= row + WINDOW) & (col >= low)


def head_probs(query, keys, allowed):
    scores = dot_t(query, keys) * SCALE
    masked = jnp.where(allowed, scores, NEG_FILL)
    top = jnp.max(masked, axis=-1, keepdims=True)
    powers = jnp.exp(masked - top)
    return powers / jnp.sum(powers, axis=-1, keepdims=True)


def attend_fwd_body(sequences, positions, window_rows, shards, meta_ref, q_ref, kv_ref, pw_ref, o_ref, keys_ref):
    load_window(meta_ref, kv_ref, pw_ref, keys_ref, sequences, positions, window_rows, shards)
    allowed = window_mask(meta_ref, positions)
    for a in range(KEY_VALUE_HEADS):
        keys = keys_ref[:, a * HEAD_DIM : (a + 1) * HEAD_DIM]
        vals = keys_ref[:, KEY_WIDTH + a * HEAD_DIM : KEY_WIDTH + (a + 1) * HEAD_DIM]
        for g in range(HEADS_PER_KEY):
            c = a * HEADS_PER_KEY + g
            probs = head_probs(q_ref[:, c * HEAD_DIM : (c + 1) * HEAD_DIM], keys, allowed)
            o_ref[:, c * HEAD_DIM : (c + 1) * HEAD_DIM] = to_low(dot(to_low(probs), vals))


def attend_bwd_body(
    sequences, positions, window_rows, shards,
    meta_ref, q_ref, kv_ref, pw_ref, go_ref, gq_ref, gkv_ref, gpw_ref, keys_ref, grads_ref,
):
    load_window(meta_ref, kv_ref, pw_ref, keys_ref, sequences, positions, window_rows, shards)
    allowed = window_mask(meta_ref, positions)
    for a in range(KEY_VALUE_HEADS):
        keys = keys_ref[:, a * HEAD_DIM : (a + 1) * HEAD_DIM]
        vals = keys_ref[:, KEY_WIDTH + a * HEAD_DIM : KEY_WIDTH + (a + 1) * HEAD_DIM]
        grad_keys = jnp.zeros((WINDOW + positions, HEAD_DIM), F32)
        grad_vals = jnp.zeros((WINDOW + positions, HEAD_DIM), F32)
        for g in range(HEADS_PER_KEY):
            c = a * HEADS_PER_KEY + g
            query = q_ref[:, c * HEAD_DIM : (c + 1) * HEAD_DIM]
            grad_out = go_ref[:, c * HEAD_DIM : (c + 1) * HEAD_DIM]
            probs = head_probs(query, keys, allowed)
            grad_probs = dot_t(grad_out, vals)
            delta = jnp.sum(probs * grad_probs, axis=-1, keepdims=True)
            grad_scores = to_low(probs * (grad_probs - delta))
            gq_ref[:, c * HEAD_DIM : (c + 1) * HEAD_DIM] = dot(grad_scores, keys) * SCALE
            grad_keys = grad_keys + t_dot(grad_scores, query)
            grad_vals = grad_vals + t_dot(to_low(probs), grad_out)
        grads_ref[:, a * HEAD_DIM : (a + 1) * HEAD_DIM] = to_low(grad_keys * SCALE)
        grads_ref[:, KEY_WIDTH + a * HEAD_DIM : KEY_WIDTH + (a + 1) * HEAD_DIM] = to_low(grad_vals)
    gkv_ref[...] = jnp.zeros_like(gkv_ref)
    gpw_ref[...] = jnp.zeros_like(gpw_ref)
    blocks = WINDOW // positions + 1
    per_block = positions // window_rows
    for b in range(blocks):
        slot = meta_ref[sequences + b]

        @pl.when(slot >= 0)
        def _():
            gkv_ref[jnp.maximum(slot, 0), 0] = grads_ref[b * positions : (b + 1) * positions, :]

        @pl.when(slot < 0)
        def _():
            for m in range(per_block):
                piece = meta_ref[sequences + blocks + b * per_block + m]
                at = b * positions + m * window_rows
                gpw_ref[piece, 0] = grads_ref[at : at + window_rows, :]


def attention_specs(sequences, positions, window_rows, shards):
    rows = pl.BlockSpec((positions, QUERY_WIDTH), lambda i, m: (i, 0))
    kv = pl.BlockSpec((shards, 1, positions, 2 * KEY_WIDTH), lambda i, m: (0, i, 0, 0))
    pw = pl.BlockSpec((shards, 1, window_rows, 2 * KEY_WIDTH), lambda i, m: (0, i, 0, 0))
    return rows, kv, pw


def attend_fwd(meta, query, kv_slots, pw_slots, dims):
    sequences, positions, window_rows, shards = dims
    rows, kv, pw = attention_specs(*dims)
    return pl.pallas_call(
        lambda *refs: attend_fwd_body(*dims, *refs),
        grid_spec=pltpu.PrefetchScalarGridSpec(
            num_scalar_prefetch=1,
            grid=(sequences,),
            in_specs=[rows, kv, pw],
            out_specs=rows,
            scratch_shapes=[pltpu.VMEM((WINDOW + positions, 2 * KEY_WIDTH), BF16)],
        ),
        out_shape=jax.ShapeDtypeStruct((sequences * positions, QUERY_WIDTH), BF16),
        name="attend_fwd",
    )(meta, query, kv_slots, pw_slots)


def attend_bwd(meta, query, kv_slots, pw_slots, grad_out, dims):
    sequences, positions, window_rows, shards = dims
    rows, kv, pw = attention_specs(*dims)
    return pl.pallas_call(
        lambda *refs: attend_bwd_body(*dims, *refs),
        grid_spec=pltpu.PrefetchScalarGridSpec(
            num_scalar_prefetch=1,
            grid=(sequences,),
            in_specs=[rows, kv, pw, rows],
            out_specs=[rows, kv, pw],
            scratch_shapes=[
                pltpu.VMEM((WINDOW + positions, 2 * KEY_WIDTH), BF16),
                pltpu.VMEM((WINDOW + positions, 2 * KEY_WIDTH), BF16),
            ],
        ),
        out_shape=[
            jax.ShapeDtypeStruct((sequences * positions, QUERY_WIDTH), F32),
            jax.ShapeDtypeStruct(kv_slots.shape, BF16),
            jax.ShapeDtypeStruct(pw_slots.shape, BF16),
        ],
        name="attend_bwd",
    )(meta, query, kv_slots, pw_slots, grad_out)


def on_device(
    tokens,
    layer_input,
    cotangent,
    lengths,
    deal_order,
    attention_input_weight,
    attn_out,
    gate_up,
    ffn_down,
    laurel_pair,
    layer_pair,
    norm_gains,
    head_gains,
):
    sequences, positions, model_width = tokens.shape
    plane = lax.axis_index("rep")
    shard = lax.axis_index("fsdp")
    planes = lax.axis_size("rep")
    shards = lax.axis_size("fsdp")
    rows_here = sequences * positions
    window_rows = WINDOW // shards
    width_here = model_width // shards
    dims = (sequences, positions, window_rows, shards)
    over_fsdp = Exchange("fsdp", fsdp_phases(shards), shards)
    over_rep = Exchange("rep", rep_phases(planes), planes)

    in_w = lax.all_gather(attention_input_weight, "fsdp", axis=0, tiled=True)
    gate_w = lax.all_to_all(gate_up[:, :HIDDEN_UNITS], "fsdp", split_axis=1, concat_axis=0, tiled=True)
    up_w = lax.all_to_all(gate_up[:, HIDDEN_UNITS:], "fsdp", split_axis=1, concat_axis=0, tiled=True)
    down_w = lax.all_to_all(ffn_down, "fsdp", split_axis=1, concat_axis=0, tiled=True)
    small = jnp.concatenate([attn_out, laurel_pair, layer_pair], axis=1)
    small_w = lax.all_gather(small, "fsdp", axis=0, tiled=True)
    out_w = small_w[:, :QUERY_WIDTH]
    laurel_w = small_w[:, QUERY_WIDTH : QUERY_WIDTH + 2 * RESIDUAL_RANK]
    layer_w = small_w[:, QUERY_WIDTH + 2 * RESIDUAL_RANK :]
    gains_w = lax.all_gather(norm_gains, "fsdp", axis=1, tiled=True)
    scales = gains_w.astype(F32)
    head_scales = head_gains.astype(F32)

    count = deal_order.shape[0]
    ids = jnp.arange(count, dtype=jnp.int32)
    takes = deal_order[None, :] == ids[:, None]
    slot_of = jnp.sum(jnp.where(takes, ids[None, :], 0), axis=1)
    slot_lens = jnp.sum(jnp.where(takes, lengths[:, None], 0), axis=0)
    earlier = (ids[None, :] < ids[:, None]) & (ids[None, :] // sequences == ids[:, None] // sequences)
    slot_offsets = jnp.sum(jnp.where(earlier, slot_lens[None, :], 0), axis=1)
    offset_of = jnp.sum(jnp.where(takes, slot_offsets[None, :], 0), axis=1)
    group_of = slot_of // sequences
    home_offset = lax.dynamic_slice_in_dim(offset_of, plane * sequences, sequences)
    home_group = lax.dynamic_slice_in_dim(group_of, plane * sequences, sequences)
    home_length = lax.dynamic_slice_in_dim(lengths, plane * sequences, sequences)
    at_position = shard * positions + jnp.arange(positions, dtype=jnp.int32)
    stream = (home_offset[:, None] + at_position[None, :]).reshape(rows_here)
    live = (at_position[None, :] < home_length[:, None]).astype(F32).reshape(rows_here, 1)
    angles = stream.astype(F32)[:, None] * frequencies()[None, :]
    cosine, sine = lax.optimization_barrier((jnp.cos(angles), jnp.sin(angles)))

    far = 1 << 14
    fsdp_sources = over_fsdp.sources(shard)
    fsdp_slots = over_fsdp.slots(shard)
    rep_sources = over_rep.sources(plane)
    target = (rep_sources[:, None] * sequences + jnp.arange(sequences, dtype=jnp.int32)[None, :]).reshape(-1)
    picks = target[:, None] == ids[None, :]
    target_base = jnp.sum(jnp.where(picks, (group_of * far + offset_of)[None, :], 0), axis=1)
    window_at = shard * window_rows - WINDOW + jnp.arange(window_rows, dtype=jnp.int32)
    target_key = (target_base[:, None] + window_at[None, :]).reshape(-1)
    source_position = fsdp_sources[:, None] * positions + jnp.arange(positions, dtype=jnp.int32)[None, :]
    source_key = jnp.where(
        source_position[:, None, :] < home_length[None, :, None],
        (home_group * far + home_offset)[None, :, None] + source_position[:, None, :],
        -(1 << 20),
    ).reshape(-1)
    window_pick = (target_key[:, None] == source_key[None, :]).astype(BF16)

    blocks = WINDOW // positions + 1
    block_device = shard - (blocks - 1) + jnp.arange(blocks, dtype=jnp.int32)
    device_slot = jnp.sum(
        jnp.where(block_device[:, None] == jnp.arange(shards, dtype=jnp.int32)[None, :], fsdp_slots[None, :], 0),
        axis=1,
    )
    block_slot = jnp.where(block_device >= 0, device_slot, -1)
    pieces = (blocks) * (positions // window_rows)
    piece_index = jnp.clip(
        shard * (positions // window_rows) + jnp.arange(pieces, dtype=jnp.int32), 0, shards - 1
    )
    piece_slot = jnp.sum(
        jnp.where(piece_index[:, None] == jnp.arange(shards, dtype=jnp.int32)[None, :], fsdp_slots[None, :], 0),
        axis=1,
    )
    low = WINDOW - home_offset - shard * positions
    meta = jnp.concatenate([low, block_slot, piece_slot]).astype(jnp.int32)

    x_float = tokens.reshape(rows_here, model_width).astype(F32)
    layer_float = layer_input.reshape(rows_here, PER_LAYER_WIDTH).astype(F32)
    hidden = rms_norm(x_float, scales[0])
    hidden_b = to_low(hidden)
    qkv = dot(hidden_b, in_w)
    query_b, kv_b = heads_fwd(qkv, cosine, sine, head_scales, positions)
    kv_slots = over_fsdp.gather(kv_b.reshape(sequences, positions, 2 * KEY_WIDTH))
    plane_kv = kv_slots.reshape(shards * rows_here, 2 * KEY_WIDTH)
    window_part = to_low(dot(window_pick, plane_kv)).reshape(planes * sequences, window_rows, 2 * KEY_WIDTH)
    pw_slots = over_fsdp.gather(over_rep.scatter(window_part))
    kv_slots = kv_slots.reshape(shards, sequences, positions, 2 * KEY_WIDTH)
    pw_slots = pw_slots.reshape(shards, sequences, window_rows, 2 * KEY_WIDTH)
    attended_b = attend_fwd(meta, query_b, kv_slots, pw_slots, dims)
    attn_proj = dot_t(attended_b, out_w)
    laurel_mid_b = to_low(dot(hidden_b, laurel_w[:, :RESIDUAL_RANK]))
    laurel_back = dot_t(laurel_mid_b, laurel_w[:, RESIDUAL_RANK:])
    first_sum = combine(x_float, attn_proj, laurel_back, hidden, scales[1], scales[2])
    ffn_in_b = to_low(rms_norm(first_sum, scales[3]))

    cot_float = cotangent.reshape(rows_here, model_width).astype(F32) * live
    chunks = []
    for i in range(sequences):
        rows = slice(i * positions, (i + 1) * positions)
        ffn_in = over_fsdp.gather(ffn_in_b[rows])
        gate = dot(ffn_in, gate_w)
        up = dot(ffn_in, up_w)
        act_b = to_low(gated(gate, up))
        down_vals = over_fsdp.scatter(to_low(dot_t(act_b, down_w))).astype(F32)
        second_sum = residual_norm(first_sum[rows], down_vals, scales[4])
        second_b = to_low(second_sum)
        layer_gate = dot(second_b, layer_w[:, :PER_LAYER_WIDTH])
        layer_mix_b = to_low(gated(layer_gate, layer_float[rows]))
        layer_back = dot_t(layer_mix_b, layer_w[:, PER_LAYER_WIDTH:])
        output, pull_out = jax.vjp(residual_norm, second_sum, layer_back, scales[5])
        mixed = to_low(output * live[rows])
        grad_second, grad_layer_back, gain_five = pull_out(cot_float[rows])
        grad_back_b = to_low(grad_layer_back)
        grad_mix = to_low(dot(grad_back_b, layer_w[:, PER_LAYER_WIDTH:])).astype(F32)
        unused_act, pull_act = jax.vjp(gated, layer_gate, layer_float[rows])
        grad_gate_layer, grad_layer_in = pull_act(grad_mix)
        grad_gate_b = to_low(grad_gate_layer)
        grad_second = grad_second + dot_t(grad_gate_b, layer_w[:, :PER_LAYER_WIDTH])
        unused_mid, pull_mid = jax.vjp(residual_norm, first_sum[rows], down_vals, scales[4])
        grad_first, grad_down, gain_four = pull_mid(grad_second)
        grad_down_all = over_fsdp.gather(to_low(grad_down))
        grad_act = to_low(dot(grad_down_all, down_w)).astype(F32)
        unused_ffn, pull_ffn = jax.vjp(gated, gate, up)
        grad_gate, grad_up = pull_ffn(grad_act)
        grad_gate_h = to_low(grad_gate)
        grad_up_h = to_low(grad_up)
        grad_in_part = to_low(dot_t(grad_gate_h, gate_w) + dot_t(grad_up_h, up_w))
        grad_ffn_in = over_fsdp.scatter(grad_in_part).astype(F32)
        unused_pre, pull_pre = jax.vjp(rms_norm, first_sum[rows], scales[3])
        grad_first_b, gain_three = pull_pre(grad_ffn_in)
        chunks.append(
            dict(
                mixed=mixed,
                grad_layer_in=to_low(grad_layer_in),
                grad_first=grad_first + grad_first_b,
                ffn_in=ffn_in,
                act=act_b,
                grad_down=grad_down_all,
                grad_gate=grad_gate_h,
                grad_up=grad_up_h,
                second=second_b,
                grad_gate_layer=grad_gate_b,
                grad_back=grad_back_b,
                layer_mix=layer_mix_b,
                gains=(gain_three, gain_four, gain_five),
            )
        )

    def joined(name):
        return jnp.concatenate([c[name] for c in chunks], axis=0)

    def own_rows(grad):
        wide = to_low(grad).reshape(shards, planes, width_here // planes, grad.shape[1])
        ordered = jnp.concatenate(
            [lax.dynamic_slice_in_dim(wide, rep_sources[q], 1, 1) for q in range(planes)], axis=1
        )
        ordered = jnp.moveaxis(ordered, 1, 0).reshape(planes, shards * (width_here // planes), grad.shape[1])
        mine = over_rep.scatter(ordered)[0]
        theirs = lax.all_to_all(mine, "fsdp", split_axis=0, concat_axis=1, tiled=True)
        return lax.all_gather(theirs, "rep", axis=0, tiled=True)

    ffn_in_all = joined("ffn_in")
    down_grad = own_rows(t_dot(joined("grad_down"), joined("act")))
    gate_grad = own_rows(t_dot(ffn_in_all, joined("grad_gate")))
    up_grad = own_rows(t_dot(ffn_in_all, joined("grad_up")))
    gate_up_grad = jnp.concatenate([gate_grad, up_grad], axis=1).astype(F32)
    ffn_down_grad = down_grad.astype(F32)

    grad_first = joined("grad_first")
    unused_comb, pull_combine = jax.vjp(
        combine, x_float, attn_proj, laurel_back, hidden, scales[1], scales[2]
    )
    grad_x_one, grad_proj, grad_laurel, grad_hidden, gain_one, gain_two = pull_combine(grad_first)
    grad_proj_b = to_low(grad_proj)
    grad_laurel_b = to_low(grad_laurel)
    grad_mid_b = to_low(dot(grad_laurel_b, laurel_w[:, RESIDUAL_RANK:]))
    grad_attended_b = to_low(dot(grad_proj_b, out_w))
    grad_query, gkv_part, gpw_part = attend_bwd(meta, query_b, kv_slots, pw_slots, grad_attended_b, dims)
    gpw_here = over_fsdp.scatter(gpw_part.reshape(shards * sequences, window_rows, 2 * KEY_WIDTH))
    gpw_all = over_rep.gather(gpw_here).reshape(-1, 2 * KEY_WIDTH)
    gkv_sum = t_dot(window_pick, gpw_all) + gkv_part.reshape(-1, 2 * KEY_WIDTH).astype(F32)
    grad_kv = over_fsdp.scatter(to_low(gkv_sum).reshape(shards * sequences, positions, 2 * KEY_WIDTH))
    grad_qkv_b, grad_head = heads_bwd(
        qkv, cosine, sine, head_scales, grad_query, grad_kv.reshape(rows_here, 2 * KEY_WIDTH), positions
    )
    grad_hidden = (
        grad_hidden + dot_t(grad_mid_b, laurel_w[:, :RESIDUAL_RANK]) + dot_t(grad_qkv_b, in_w)
    )
    unused_norm, pull_in = jax.vjp(rms_norm, x_float, scales[0])
    grad_x_two, gain_zero = pull_in(grad_hidden)
    input_grad = to_low(grad_x_one + grad_x_two).reshape(tokens.shape)

    small_part = jnp.concatenate(
        [
            to_low(t_dot(grad_proj_b, attended_b)),
            to_low(t_dot(hidden_b, grad_mid_b)),
            to_low(t_dot(grad_laurel_b, laurel_mid_b)),
            to_low(t_dot(joined("second"), joined("grad_gate_layer"))),
            to_low(t_dot(joined("grad_back"), joined("layer_mix"))),
        ],
        axis=1,
    )
    small_grad = lax.psum(lax.psum_scatter(small_part, "fsdp", scatter_dimension=0, tiled=True), "rep").astype(F32)
    in_part = to_low(t_dot(hidden_b, grad_qkv_b))
    attn_in_grad = lax.psum(lax.psum_scatter(in_part, "fsdp", scatter_dimension=0, tiled=True), "rep").astype(F32)

    gain_rows = jnp.stack(
        [gain_zero, gain_one, gain_two] + [sum(c["gains"][k] for c in chunks) for k in range(3)]
    )
    packed = jnp.concatenate([gain_rows, jnp.pad(grad_head, ((0, 0), (0, model_width - HEAD_DIM)))], axis=0)
    packed = over_rep.total(over_fsdp.total(packed))
    gain_share = lax.dynamic_slice_in_dim(packed[:6], shard * width_here, width_here, 1)
    return (
        jnp.stack([c["mixed"] for c in chunks]),
        input_grad,
        jnp.stack([c["grad_layer_in"] for c in chunks]),
        attn_in_grad,
        small_grad[:, :QUERY_WIDTH],
        gate_up_grad,
        ffn_down_grad,
        small_grad[:, QUERY_WIDTH : QUERY_WIDTH + 2 * RESIDUAL_RANK],
        small_grad[:, QUERY_WIDTH + 2 * RESIDUAL_RANK :],
        gain_share,
        packed[6:8, :HEAD_DIM],
    )


def solution(mesh):
    rows = P("rep", "fsdp", None)
    weight = P("fsdp", None)
    return jax.shard_map(
        on_device,
        mesh=mesh,
        in_specs=(rows, rows, rows, P(), P()) + (weight,) * 6 + (P(None, "fsdp"), P()),
        out_specs=(rows, rows, rows) + (weight,) * 6 + (P(None, "fsdp"), P()),
        check_vma=False,
    )
```

```python
import jax
import jax.numpy as jnp
import numpy as np
from jax import lax
from jax.experimental import pallas as pl
from jax.experimental.pallas import tpu as pltpu
from jax.sharding import PartitionSpec as P

QUERY_HEADS = 8
KEY_VALUE_HEADS = 2
HEADS_PER_KEY = QUERY_HEADS // KEY_VALUE_HEADS
HEAD_DIM = 256
HALF_DIM = HEAD_DIM // 2
HIDDEN_UNITS = 8192
RESIDUAL_RANK = 64
PER_LAYER_WIDTH = 256
WINDOW = 512
QUERY_WIDTH = QUERY_HEADS * HEAD_DIM
KEY_WIDTH = KEY_VALUE_HEADS * HEAD_DIM

EPS = 1e-06
BASE = 10000.0
ROOT_HALF = 0.7071067811865476
NEG_FILL = -1e30
SCALE = HEAD_DIM ** (-0.5)

F32 = jnp.float32
BF16 = jnp.bfloat16


def rms_norm(values, scales):
    return values * lax.rsqrt(jnp.mean(values * values, axis=-1, keepdims=True) + EPS) * scales


def gelu_tanh(values):
    return jax.nn.gelu(values, approximate=True)


def frequencies():
    return 1.0 / BASE ** (jnp.arange(HALF_DIM, dtype=F32) * 2.0 / HEAD_DIM)


def combine(x_float, attn_proj, laurel_back, hidden, scale_one, scale_two):
    return (
        x_float + rms_norm(attn_proj, scale_two) + hidden + rms_norm(laurel_back, scale_one)
    ) * ROOT_HALF


def gated(gate, up):
    return gelu_tanh(gate) * up


def residual_norm(base, values, scales):
    return base + rms_norm(values, scales)


def to_low(values):
    return values.astype(BF16)


def dot(left, right):
    return jnp.dot(left, right, preferred_element_type=F32)


def dot_t(left, right):
    return lax.dot_general(left, right, (((1,), (1,)), ((), ())), preferred_element_type=F32)


def t_dot(left, right):
    return lax.dot_general(left, right, (((0,), (0,)), ((), ())), preferred_element_type=F32)


def fsdp_phases(count):
    bits = [1 << k for k in range(1, count.bit_length() - 1)]
    phases = []
    for k in range(len(bits)):
        phases.append([i ^ (bits[k] if i % 2 == 0 else bits[len(bits) - 1 - k]) for i in range(count)])
    phases.append([i ^ 1 for i in range(count)])
    return phases


def rep_phases(count):
    bits = [1 << k for k in range(count.bit_length() - 1)]
    return [[i ^ b for i in range(count)] for b in reversed(bits)]


def slot_table(phases, count):
    held = [[i] for i in range(count)]
    for perm in phases:
        held = [held[i] + held[perm[i]] for i in range(count)]
    return np.array(held, dtype=np.int32).T


class Exchange:
    def __init__(self, axis, phases, count):
        self.axis = axis
        self.count = count
        self.perms = [[(i, p[i]) for i in range(count)] for p in phases]
        self.table = slot_table(phases, count)
        inverse = np.zeros_like(self.table)
        for i in range(count):
            inverse[self.table[:, i], i] = np.arange(count)
        self.inverse = inverse

    def sources(self, index):
        return lax.dynamic_index_in_dim(jnp.asarray(self.table), index, 1, keepdims=False)

    def slots(self, index):
        return lax.dynamic_index_in_dim(jnp.asarray(self.inverse), index, 1, keepdims=False)

    def pieces(self, piece):
        held = [piece]
        for perm in self.perms:
            held = held + [lax.ppermute(h, self.axis, perm) for h in held]
        return held

    def groups(self):
        return [(0, 1)] + [(1 << k, 2 << k) for k in range(len(self.perms))]

    def scatter(self, parts):
        spans = self.groups()
        for k in range(len(self.perms), 0, -1):
            got = lax.ppermute(parts[k], self.axis, self.perms[k - 1])
            step = got.shape[0] // spans[k][0]
            parts = [
                (parts[j].astype(F32) + got[spans[j][0] * step : spans[j][1] * step].astype(F32)).astype(got.dtype)
                for j in range(k)
            ]
        return parts[0]

    def scatter_whole(self, whole):
        step = whole.shape[0] // self.count
        return self.scatter([whole[lo * step : hi * step] for lo, hi in self.groups()])

    def total(self, value):
        for perm in self.perms:
            value = value + lax.ppermute(value, self.axis, perm)
        return value


class Line:
    def __init__(self, axis, count):
        self.axis = axis
        self.count = count

    def scatter(self, parts):
        count = self.count
        right = left = None
        for s in range(1, count):
            out = parts[count - s] if right is None else add_low(parts[count - s], right)
            right = lax.ppermute(out, self.axis, [(i, i + 1) for i in range(s)])
            out = parts[s] if left is None else add_low(parts[s], left)
            left = lax.ppermute(out, self.axis, [(i, i - 1) for i in range(count - s, count)])
        return (parts[0].astype(F32) + right.astype(F32) + left.astype(F32)).astype(parts[0].dtype)

    def gather(self, piece):
        count = self.count
        right, left = [piece], [piece]
        for s in range(1, count):
            right.append(lax.ppermute(right[-1], self.axis, [(i, i + 1) for i in range(s - 1, count - 1)]))
            left.append(lax.ppermute(left[-1], self.axis, [(i, i - 1) for i in range(1, count - s + 1)]))
        return [piece] + [right[count - r] + left[r] for r in range(1, count)]


def add_low(left, right):
    return (left.astype(F32) + right.astype(F32)).astype(left.dtype)


def heads_fwd_body(qkv_ref, cos_ref, sin_ref, gains_ref, q_ref, kv_ref):
    cosine = cos_ref[...]
    sine = sin_ref[...]
    for c in range(QUERY_HEADS + 2 * KEY_VALUE_HEADS):
        head = qkv_ref[:, c * HEAD_DIM : (c + 1) * HEAD_DIM]
        normed = head * lax.rsqrt(jnp.mean(head * head, axis=-1, keepdims=True) + EPS)
        if c < QUERY_HEADS + KEY_VALUE_HEADS:
            row = 0 if c < QUERY_HEADS else 1
            normed = normed * gains_ref[row : row + 1, :]
            low = normed[:, :HALF_DIM]
            high = normed[:, HALF_DIM:]
            first = to_low(low * cosine - high * sine)
            second = to_low(high * cosine + low * sine)
        else:
            first = to_low(normed[:, :HALF_DIM])
            second = to_low(normed[:, HALF_DIM:])
        if c < QUERY_HEADS:
            q_ref[:, c * HEAD_DIM : c * HEAD_DIM + HALF_DIM] = first
            q_ref[:, c * HEAD_DIM + HALF_DIM : (c + 1) * HEAD_DIM] = second
        else:
            at = (c - QUERY_HEADS) * HEAD_DIM
            kv_ref[:, at : at + HALF_DIM] = first
            kv_ref[:, at + HALF_DIM : at + HEAD_DIM] = second


def heads_fwd(qkv, cosine, sine, head_scales, block):
    rows, width = qkv.shape
    return pl.pallas_call(
        heads_fwd_body,
        grid=(rows // block,),
        in_specs=[
            pl.BlockSpec((block, width), lambda i: (i, 0)),
            pl.BlockSpec((block, HALF_DIM), lambda i: (i, 0)),
            pl.BlockSpec((block, HALF_DIM), lambda i: (i, 0)),
            pl.BlockSpec((2, HEAD_DIM), lambda i: (0, 0)),
        ],
        out_specs=[
            pl.BlockSpec((block, QUERY_WIDTH), lambda i: (i, 0)),
            pl.BlockSpec((block, 2 * KEY_WIDTH), lambda i: (i, 0)),
        ],
        out_shape=[
            jax.ShapeDtypeStruct((rows, QUERY_WIDTH), BF16),
            jax.ShapeDtypeStruct((rows, 2 * KEY_WIDTH), BF16),
        ],
        name="heads_fwd",
    )(qkv, cosine, sine, head_scales)


def heads_bwd_body(heads, gained, qkv_ref, cos_ref, sin_ref, gains_ref, grad_ref, out_ref, gain_ref):
    @pl.when(pl.program_id(0) == 0)
    def _():
        gain_ref[...] = jnp.zeros_like(gain_ref)

    cosine = cos_ref[...]
    sine = sin_ref[...]
    total = jnp.zeros((1, HEAD_DIM), F32)
    for c in range(heads):
        here = slice(c * HEAD_DIM, (c + 1) * HEAD_DIM)
        head = qkv_ref[:, here]
        scale = lax.rsqrt(jnp.mean(head * head, axis=-1, keepdims=True) + EPS)
        normed = head * scale
        grad = grad_ref[:, here].astype(F32)
        if c < gained:
            first = grad[:, :HALF_DIM]
            second = grad[:, HALF_DIM:]
            grad = jnp.concatenate(
                [first * cosine + second * sine, second * cosine - first * sine], axis=1
            )
            total = total + jnp.sum(grad * normed, axis=0, keepdims=True)
            grad = grad * gains_ref[...]
        back = scale * (grad - normed * jnp.mean(grad * normed, axis=-1, keepdims=True))
        out_ref[:, here] = to_low(back)
    gain_ref[...] += total


def heads_bwd(qkv, first, heads, gained, cosine, sine, head_scale, grad, block):
    rows = qkv.shape[0]
    width = heads * HEAD_DIM
    at = first // heads
    return pl.pallas_call(
        lambda *refs: heads_bwd_body(heads, gained, *refs),
        grid=(rows // block,),
        in_specs=[
            pl.BlockSpec((block, width), lambda i: (i, at)),
            pl.BlockSpec((block, HALF_DIM), lambda i: (i, 0)),
            pl.BlockSpec((block, HALF_DIM), lambda i: (i, 0)),
            pl.BlockSpec((1, HEAD_DIM), lambda i: (0, 0)),
            pl.BlockSpec((block, width), lambda i: (i, 0)),
        ],
        out_specs=[
            pl.BlockSpec((block, width), lambda i: (i, 0)),
            pl.BlockSpec((1, HEAD_DIM), lambda i: (0, 0)),
        ],
        out_shape=[
            jax.ShapeDtypeStruct((rows, width), BF16),
            jax.ShapeDtypeStruct((1, HEAD_DIM), F32),
        ],
        name="heads_bwd",
    )(qkv, cosine, sine, head_scale, grad)


def load_window(meta_ref, kv_ref, pw_ref, keys_ref, sequences, positions, window_rows, shards):
    blocks = WINDOW // positions + 1
    per_block = positions // window_rows
    for b in range(blocks):
        slot = meta_ref[sequences + b]

        @pl.when(slot >= 0)
        def _():
            keys_ref[b * positions : (b + 1) * positions, :] = kv_ref[jnp.maximum(slot, 0), 0]

        @pl.when(slot < 0)
        def _():
            for m in range(per_block):
                piece = meta_ref[sequences + blocks + b * per_block + m]
                at = b * positions + m * window_rows
                keys_ref[at : at + window_rows, :] = pw_ref[piece, 0]


def window_mask(meta_ref, positions):
    width = WINDOW + positions
    row = lax.broadcasted_iota(jnp.int32, (positions, width), 0)
    col = lax.broadcasted_iota(jnp.int32, (positions, width), 1)
    low = meta_ref[pl.program_id(0)]
    return (col > row) & (col <= row + WINDOW) & (col >= low)


def head_probs(query, keys, allowed):
    scores = dot_t(query, keys) * SCALE
    masked = jnp.where(allowed, scores, NEG_FILL)
    top = jnp.max(masked, axis=-1, keepdims=True)
    powers = jnp.exp(masked - top)
    return powers / jnp.sum(powers, axis=-1, keepdims=True)


def attend_fwd_body(sequences, positions, window_rows, shards, meta_ref, q_ref, kv_ref, pw_ref, o_ref, keys_ref):
    load_window(meta_ref, kv_ref, pw_ref, keys_ref, sequences, positions, window_rows, shards)
    allowed = window_mask(meta_ref, positions)
    for a in range(KEY_VALUE_HEADS):
        keys = keys_ref[:, a * HEAD_DIM : (a + 1) * HEAD_DIM]
        vals = keys_ref[:, KEY_WIDTH + a * HEAD_DIM : KEY_WIDTH + (a + 1) * HEAD_DIM]
        for g in range(HEADS_PER_KEY):
            c = a * HEADS_PER_KEY + g
            probs = head_probs(q_ref[:, c * HEAD_DIM : (c + 1) * HEAD_DIM], keys, allowed)
            o_ref[:, c * HEAD_DIM : (c + 1) * HEAD_DIM] = to_low(dot(to_low(probs), vals))


def attend_bwd_body(
    sequences, positions, window_rows, shards,
    meta_ref, q_ref, kv_ref, pw_ref, go_ref, gq_ref, gkv_ref, gpw_ref, keys_ref, grads_ref,
):
    load_window(meta_ref, kv_ref, pw_ref, keys_ref, sequences, positions, window_rows, shards)
    allowed = window_mask(meta_ref, positions)
    for a in range(KEY_VALUE_HEADS):
        keys = keys_ref[:, a * HEAD_DIM : (a + 1) * HEAD_DIM]
        vals = keys_ref[:, KEY_WIDTH + a * HEAD_DIM : KEY_WIDTH + (a + 1) * HEAD_DIM]
        grad_keys = jnp.zeros((WINDOW + positions, HEAD_DIM), F32)
        grad_vals = jnp.zeros((WINDOW + positions, HEAD_DIM), F32)
        for g in range(HEADS_PER_KEY):
            c = a * HEADS_PER_KEY + g
            query = q_ref[:, c * HEAD_DIM : (c + 1) * HEAD_DIM]
            grad_out = go_ref[:, c * HEAD_DIM : (c + 1) * HEAD_DIM]
            probs = head_probs(query, keys, allowed)
            grad_probs = dot_t(grad_out, vals)
            delta = jnp.sum(probs * grad_probs, axis=-1, keepdims=True)
            grad_scores = to_low(probs * (grad_probs - delta))
            gq_ref[:, c * HEAD_DIM : (c + 1) * HEAD_DIM] = dot(grad_scores, keys) * SCALE
            grad_keys = grad_keys + t_dot(grad_scores, query)
            grad_vals = grad_vals + t_dot(to_low(probs), grad_out)
        grads_ref[:, a * HEAD_DIM : (a + 1) * HEAD_DIM] = to_low(grad_keys * SCALE)
        grads_ref[:, KEY_WIDTH + a * HEAD_DIM : KEY_WIDTH + (a + 1) * HEAD_DIM] = to_low(grad_vals)
    gkv_ref[...] = jnp.zeros_like(gkv_ref)
    gpw_ref[...] = jnp.zeros_like(gpw_ref)
    blocks = WINDOW // positions + 1
    per_block = positions // window_rows
    for b in range(blocks):
        slot = meta_ref[sequences + b]

        @pl.when(slot >= 0)
        def _():
            gkv_ref[jnp.maximum(slot, 0), 0] = grads_ref[b * positions : (b + 1) * positions, :]

        @pl.when(slot < 0)
        def _():
            for m in range(per_block):
                piece = meta_ref[sequences + blocks + b * per_block + m]
                at = b * positions + m * window_rows
                gpw_ref[piece, 0] = grads_ref[at : at + window_rows, :]


def attention_specs(sequences, positions, window_rows, shards):
    rows = pl.BlockSpec((positions, QUERY_WIDTH), lambda i, m: (i, 0))
    kv = pl.BlockSpec((shards, 1, positions, 2 * KEY_WIDTH), lambda i, m: (0, i, 0, 0))
    pw = pl.BlockSpec((shards, 1, window_rows, 2 * KEY_WIDTH), lambda i, m: (0, i, 0, 0))
    return rows, kv, pw


def attend_fwd(meta, query, kv_slots, pw_slots, dims):
    sequences, positions, window_rows, shards = dims
    rows, kv, pw = attention_specs(*dims)
    return pl.pallas_call(
        lambda *refs: attend_fwd_body(*dims, *refs),
        grid_spec=pltpu.PrefetchScalarGridSpec(
            num_scalar_prefetch=1,
            grid=(sequences,),
            in_specs=[rows, kv, pw],
            out_specs=rows,
            scratch_shapes=[pltpu.VMEM((WINDOW + positions, 2 * KEY_WIDTH), BF16)],
        ),
        out_shape=jax.ShapeDtypeStruct((sequences * positions, QUERY_WIDTH), BF16),
        name="attend_fwd",
    )(meta, query, kv_slots, pw_slots)


def attend_bwd(meta, query, kv_slots, pw_slots, grad_out, dims):
    sequences, positions, window_rows, shards = dims
    rows, kv, pw = attention_specs(*dims)
    return pl.pallas_call(
        lambda *refs: attend_bwd_body(*dims, *refs),
        grid_spec=pltpu.PrefetchScalarGridSpec(
            num_scalar_prefetch=1,
            grid=(sequences,),
            in_specs=[rows, kv, pw, rows],
            out_specs=[rows, kv, pw],
            scratch_shapes=[
                pltpu.VMEM((WINDOW + positions, 2 * KEY_WIDTH), BF16),
                pltpu.VMEM((WINDOW + positions, 2 * KEY_WIDTH), BF16),
            ],
        ),
        out_shape=[
            jax.ShapeDtypeStruct((sequences * positions, QUERY_WIDTH), F32),
            jax.ShapeDtypeStruct(kv_slots.shape, BF16),
            jax.ShapeDtypeStruct(pw_slots.shape, BF16),
        ],
        name="attend_bwd",
    )(meta, query, kv_slots, pw_slots, grad_out)


GELU_A = 0.7978845608028654
GELU_B = 0.044715


def write_groups(acc_ref, out_refs, rows):
    start = 0
    for ref in out_refs:
        size = ref.shape[0]
        ref[...] = to_low(acc_ref[start : start + size, :])
        start += size


def ffn_fwd_body(shards, *refs):
    x_refs = refs[:shards]
    gate_ref, up_ref, down_ref = refs[shards : shards + 3]
    act_ref, slope_ref, value_ref, all_ref = refs[shards + 3 : shards + 7]
    out_refs = refs[shards + 7 : -1]
    acc_ref = refs[-1]
    rows = x_refs[0].shape[0]
    step = pl.program_id(0)

    @pl.when(step == 0)
    def _():
        for k in range(shards):
            all_ref[k * rows : (k + 1) * rows, :] = x_refs[k][...]

    part = (shards * rows) // 4
    for k in range(4):
        here = slice(k * part, (k + 1) * part)
        inputs = all_ref[here, :]
        gate = dot(inputs, gate_ref[...])
        up = dot(inputs, up_ref[...])
        squared = gate * gate
        bend = jnp.tanh(GELU_A * gate * (1.0 + GELU_B * squared))
        half = 0.5 * (1.0 + bend)
        value = gate * half
        slope = half + (0.5 * GELU_A) * gate * (1.0 - bend * bend) * (1.0 + 3.0 * GELU_B * squared)
        act = to_low(value * up)
        act_ref[here, :] = act
        slope_ref[here, :] = to_low(slope * up)
        value_ref[here, :] = to_low(value)
        down = dot_t(act, down_ref[...])

        @pl.when(step == 0)
        def _():
            acc_ref[here, :] = down

        @pl.when(step > 0)
        def _():
            acc_ref[here, :] += down

    @pl.when(step == pl.num_programs(0) - 1)
    def _():
        write_groups(acc_ref, out_refs, rows)


def weight_specs(width, hidden, block):
    count = hidden // block
    return [pl.BlockSpec((width, block), lambda j, k=k: (0, k * count + j)) for k in range(3)]


def ffn_fwd(pieces, weights, spans):
    shards = len(pieces)
    rows, width = pieces[0].shape
    hidden = weights.shape[1] // 3
    block = 256
    every = shards * rows
    whole = pl.BlockSpec((rows, width), lambda j: (0, 0))
    column = pl.BlockSpec((every, block), lambda j: (0, j))
    sizes = [(hi - lo) * rows for lo, hi in spans]
    outs = pl.pallas_call(
        lambda *refs: ffn_fwd_body(shards, *refs),
        grid=(hidden // block,),
        in_specs=[whole] * shards + weight_specs(width, hidden, block),
        out_specs=[column] * 3
        + [pl.BlockSpec((every, width), lambda j: (0, 0))]
        + [pl.BlockSpec((n, width), lambda j: (0, 0)) for n in sizes],
        out_shape=[jax.ShapeDtypeStruct((every, hidden), BF16)] * 3
        + [jax.ShapeDtypeStruct((every, width), BF16)]
        + [jax.ShapeDtypeStruct((n, width), BF16) for n in sizes],
        scratch_shapes=[pltpu.VMEM((every, width), F32)],
        compiler_params=pltpu.CompilerParams(vmem_limit_bytes=60 << 20),
        cost_estimate=pl.CostEstimate(
            flops=6 * every * width * hidden, transcendentals=every * hidden,
            bytes_accessed=2 * (3 * width * hidden + 3 * every * width + 3 * every * hidden),
        ),
        name="ffn_fwd",
    )(*pieces, weights, weights, weights)
    return outs[:3], outs[3], outs[4:]


def ffn_bwd_body(shards, *refs):
    g_refs = refs[:shards]
    gate_ref, up_ref, down_ref, slope_ref, value_ref = refs[shards : shards + 5]
    gg_ref, gu_ref, all_ref = refs[shards + 5 : shards + 8]
    out_refs = refs[shards + 8 : -1]
    acc_ref = refs[-1]
    rows = g_refs[0].shape[0]
    step = pl.program_id(0)

    @pl.when(step == 0)
    def _():
        for k in range(shards):
            all_ref[k * rows : (k + 1) * rows, :] = g_refs[k][...]

    part = (shards * rows) // 4
    for k in range(4):
        here = slice(k * part, (k + 1) * part)
        grad = to_low(dot(all_ref[here, :], down_ref[...])).astype(F32)
        grad_gate = to_low(grad * slope_ref[here, :].astype(F32))
        grad_up = to_low(grad * value_ref[here, :].astype(F32))
        gg_ref[here, :] = grad_gate
        gu_ref[here, :] = grad_up
        back = dot_t(grad_gate, gate_ref[...]) + dot_t(grad_up, up_ref[...])

        @pl.when(step == 0)
        def _():
            acc_ref[here, :] = back

        @pl.when(step > 0)
        def _():
            acc_ref[here, :] += back

    @pl.when(step == pl.num_programs(0) - 1)
    def _():
        write_groups(acc_ref, out_refs, rows)


def ffn_bwd(pieces, weights, slope, value, spans):
    shards = len(pieces)
    rows, width = pieces[0].shape
    hidden = weights.shape[1] // 3
    block = 256
    every = shards * rows
    whole = pl.BlockSpec((rows, width), lambda j: (0, 0))
    column = pl.BlockSpec((every, block), lambda j: (0, j))
    sizes = [(hi - lo) * rows for lo, hi in spans]
    outs = pl.pallas_call(
        lambda *refs: ffn_bwd_body(shards, *refs),
        grid=(hidden // block,),
        in_specs=[whole] * shards + weight_specs(width, hidden, block) + [column] * 2,
        out_specs=[column] * 2
        + [pl.BlockSpec((every, width), lambda j: (0, 0))]
        + [pl.BlockSpec((n, width), lambda j: (0, 0)) for n in sizes],
        out_shape=[jax.ShapeDtypeStruct((every, hidden), BF16)] * 2
        + [jax.ShapeDtypeStruct((every, width), BF16)]
        + [jax.ShapeDtypeStruct((n, width), BF16) for n in sizes],
        scratch_shapes=[pltpu.VMEM((every, width), F32)],
        compiler_params=pltpu.CompilerParams(vmem_limit_bytes=60 << 20),
        cost_estimate=pl.CostEstimate(
            flops=6 * every * width * hidden, transcendentals=0,
            bytes_accessed=2 * (3 * width * hidden + 3 * every * width + 4 * every * hidden),
        ),
        name="ffn_bwd",
    )(*pieces, weights, weights, weights, slope, value)
    return outs[0], outs[1], outs[2], outs[3:]


def rows_grad_body(planes, count, kinds, order_ref, *refs):
    lefts = refs[:count]
    rights = refs[count : count + count * kinds]
    outs = refs[count + count * kinds :]
    for k in range(kinds):
        total = t_dot(lefts[0][...], rights[k * count][...])
        for c in range(1, count):
            total = total + t_dot(lefts[c][...], rights[k * count + c][...])
        total = to_low(total)
        rows = total.shape[0] // planes
        for q in range(planes):
            outs[k][order_ref[q], 0] = total[q * rows : (q + 1) * rows, :]


def rows_grad(order, lefts, kinds, planes, shards):
    count = len(lefts)
    rows, width = lefts[0].shape
    block = width // shards
    flat = [r for rights in kinds for r in rights]
    hidden = flat[0].shape[1]
    part = block // planes
    return pl.pallas_call(
        lambda *refs: rows_grad_body(planes, count, len(kinds), *refs),
        grid_spec=pltpu.PrefetchScalarGridSpec(
            num_scalar_prefetch=1,
            grid=(shards,),
            in_specs=[pl.BlockSpec((rows, block), lambda f, o: (0, f))] * count
            + [pl.BlockSpec((rows, hidden), lambda f, o: (0, 0))] * len(flat),
            out_specs=[pl.BlockSpec((planes, 1, part, hidden), lambda f, o: (0, f, 0, 0))] * len(kinds),
        ),
        out_shape=[jax.ShapeDtypeStruct((planes, shards, part, hidden), BF16)] * len(kinds),
        compiler_params=pltpu.CompilerParams(vmem_limit_bytes=60 << 20),
        cost_estimate=pl.CostEstimate(
            flops=2 * count * len(kinds) * rows * width * hidden, transcendentals=0,
            bytes_accessed=2 * (count * rows * width + len(flat) * rows * hidden + len(kinds) * width * hidden),
        ),
        name="rows_grad",
    )(order, *lefts, *flat)


def owner_grad_body(pairs, spans, order_ref, *refs):
    lefts = refs[: len(pairs)]
    rights = refs[len(pairs) : 2 * len(pairs)]
    outs = refs[2 * len(pairs) :]
    step = pl.program_id(0)
    for ref, (lo, hi) in zip(outs, spans):

        @pl.when((step >= lo) & (step < hi))
        def _():
            at = 0
            parts = []
            for n, (left, right) in enumerate(zip(lefts, rights)):
                value = t_dot(left[...], right[...])
                if pairs[n]:
                    parts[-1] = parts[-1] + value
                else:
                    parts.append(value)
            for value in parts:
                ref[0, :, at : at + value.shape[1]] = to_low(value)
                at += value.shape[1]


def owner_grad(order, lefts, rights, joins, spans):
    shards = spans[-1][1]
    rows, width = lefts[0].shape
    block = width // shards
    total = sum(r.shape[1] for r, j in zip(rights, joins) if not j)
    return pl.pallas_call(
        lambda *refs: owner_grad_body(joins, spans, *refs),
        grid_spec=pltpu.PrefetchScalarGridSpec(
            num_scalar_prefetch=1,
            grid=(shards,),
            in_specs=[pl.BlockSpec((rows, block), lambda t, o: (0, o[t]))] * len(lefts)
            + [pl.BlockSpec(r.shape, lambda t, o: (0, 0)) for r in rights],
            out_specs=[
                pl.BlockSpec((1, block, total), lambda t, o, lo=lo, hi=hi: (jnp.clip(t - lo, 0, hi - lo - 1), 0, 0))
                for lo, hi in spans
            ],
        ),
        out_shape=[jax.ShapeDtypeStruct((hi - lo, block, total), BF16) for lo, hi in spans],
        compiler_params=pltpu.CompilerParams(vmem_limit_bytes=60 << 20),
        cost_estimate=pl.CostEstimate(
            flops=2 * rows * width * sum(r.shape[1] for r in rights), transcendentals=0,
            bytes_accessed=2 * (rows * width * len(lefts) + rows * total + width * total),
        ),
        name="owner_grad",
    )(order, *lefts, *rights)


def on_device(
    tokens,
    layer_input,
    cotangent,
    lengths,
    deal_order,
    attention_input_weight,
    attn_out,
    gate_up,
    ffn_down,
    laurel_pair,
    layer_pair,
    norm_gains,
    head_gains,
):
    sequences, positions, model_width = tokens.shape
    plane = lax.axis_index("rep")
    shard = lax.axis_index("fsdp")
    planes = lax.axis_size("rep")
    shards = lax.axis_size("fsdp")
    rows_here = sequences * positions
    window_rows = WINDOW // shards
    width_here = model_width // shards
    dims = (sequences, positions, window_rows, shards)
    over_fsdp = Exchange("fsdp", fsdp_phases(shards), shards)
    over_rep = Exchange("rep", rep_phases(planes), planes)

    line = Line("rep", planes)
    spans = over_fsdp.groups()
    hidden_here = HIDDEN_UNITS // shards

    with jax.named_scope("gather_in"):
        in_w = lax.all_gather(attention_input_weight, "fsdp", axis=0, tiled=True)
    half_rows = width_here // 2
    lower = plane % 2 == 0

    def by_owner(part):
        return jnp.swapaxes(part.reshape(half_rows, shards, hidden_here), 0, 1)

    gate_up_half = lax.dynamic_slice_in_dim(gate_up, (plane % 2) * half_rows, half_rows, 0)
    down_half = lax.dynamic_slice_in_dim(ffn_down, (plane % 2) * half_rows, half_rows, 0)
    send = lax.optimization_barrier(
        jnp.concatenate(
            [
                by_owner(gate_up_half[:, :HIDDEN_UNITS]),
                by_owner(gate_up_half[:, HIDDEN_UNITS:]),
                by_owner(down_half),
            ],
            axis=2,
        )
    )
    with jax.named_scope("deal_ffn"):
        mine_w = lax.all_to_all(send, "fsdp", split_axis=0, concat_axis=0, tiled=True)
    with jax.named_scope("swap_ffn"):
        other_w = lax.ppermute(mine_w, "rep", [(i, i ^ 1) for i in range(planes)])
    ffn_w = jnp.stack(
        [jnp.where(lower, mine_w, other_w), jnp.where(lower, other_w, mine_w)], axis=1
    ).reshape(model_width, 3 * hidden_here)
    small = jnp.concatenate([attn_out, laurel_pair, layer_pair], axis=1)
    with jax.named_scope("gather_small"):
        small_w = lax.all_gather(small, "fsdp", axis=0, tiled=True)
    out_w = small_w[:, :QUERY_WIDTH]
    laurel_w = small_w[:, QUERY_WIDTH : QUERY_WIDTH + 2 * RESIDUAL_RANK]
    layer_w = small_w[:, QUERY_WIDTH + 2 * RESIDUAL_RANK :]
    gains_w = lax.all_gather(norm_gains, "fsdp", axis=1, tiled=True)
    scales = gains_w.astype(F32)
    head_scales = head_gains.astype(F32)

    count = deal_order.shape[0]
    ids = jnp.arange(count, dtype=jnp.int32)
    takes = deal_order[None, :] == ids[:, None]
    slot_of = jnp.sum(jnp.where(takes, ids[None, :], 0), axis=1)
    slot_lens = jnp.sum(jnp.where(takes, lengths[:, None], 0), axis=0)
    earlier = (ids[None, :] < ids[:, None]) & (ids[None, :] // sequences == ids[:, None] // sequences)
    slot_offsets = jnp.sum(jnp.where(earlier, slot_lens[None, :], 0), axis=1)
    offset_of = jnp.sum(jnp.where(takes, slot_offsets[None, :], 0), axis=1)
    group_of = slot_of // sequences
    home_offset = lax.dynamic_slice_in_dim(offset_of, plane * sequences, sequences)
    home_group = lax.dynamic_slice_in_dim(group_of, plane * sequences, sequences)
    home_length = lax.dynamic_slice_in_dim(lengths, plane * sequences, sequences)
    at_position = shard * positions + jnp.arange(positions, dtype=jnp.int32)
    stream = (home_offset[:, None] + at_position[None, :]).reshape(rows_here)
    live = (at_position[None, :] < home_length[:, None]).astype(F32).reshape(rows_here, 1)
    angles = stream.astype(F32)[:, None] * frequencies()[None, :]
    cosine, sine = lax.optimization_barrier((jnp.cos(angles), jnp.sin(angles)))

    far = 1 << 14
    fsdp_sources = over_fsdp.sources(shard)
    fsdp_slots = over_fsdp.slots(shard)
    plane_order = (plane + jnp.arange(planes, dtype=jnp.int32)) % planes
    target = (plane_order[:, None] * sequences + jnp.arange(sequences, dtype=jnp.int32)[None, :]).reshape(-1)
    picks = target[:, None] == ids[None, :]
    target_base = jnp.sum(jnp.where(picks, (group_of * far + offset_of)[None, :], 0), axis=1)
    window_at = shard * window_rows - WINDOW + jnp.arange(window_rows, dtype=jnp.int32)
    target_key = (target_base[:, None] + window_at[None, :]).reshape(-1)
    source_position = fsdp_sources[:, None] * positions + jnp.arange(positions, dtype=jnp.int32)[None, :]
    source_key = jnp.where(
        source_position[:, None, :] < home_length[None, :, None],
        (home_group * far + home_offset)[None, :, None] + source_position[:, None, :],
        -(1 << 20),
    ).reshape(-1)
    window_pick = (target_key[:, None] == source_key[None, :]).astype(BF16)

    blocks = WINDOW // positions + 1
    block_device = shard - (blocks - 1) + jnp.arange(blocks, dtype=jnp.int32)
    device_slot = jnp.sum(
        jnp.where(block_device[:, None] == jnp.arange(shards, dtype=jnp.int32)[None, :], fsdp_slots[None, :], 0),
        axis=1,
    )
    block_slot = jnp.where(block_device >= 0, device_slot, -1)
    pieces = (blocks) * (positions // window_rows)
    piece_index = jnp.clip(
        shard * (positions // window_rows) + jnp.arange(pieces, dtype=jnp.int32), 0, shards - 1
    )
    piece_slot = jnp.sum(
        jnp.where(piece_index[:, None] == jnp.arange(shards, dtype=jnp.int32)[None, :], fsdp_slots[None, :], 0),
        axis=1,
    )
    low = WINDOW - home_offset - shard * positions
    meta = jnp.concatenate([low, block_slot, piece_slot]).astype(jnp.int32)

    x_float = tokens.reshape(rows_here, model_width).astype(F32)
    layer_float = layer_input.reshape(rows_here, PER_LAYER_WIDTH).astype(F32)
    hidden = rms_norm(x_float, scales[0])
    hidden_b = to_low(hidden)
    qkv = dot(hidden_b, in_w)
    query_b, kv_b = heads_fwd(qkv, cosine, sine, head_scales, positions)
    kv_slots = jnp.concatenate(over_fsdp.pieces(kv_b.reshape(sequences, positions, 2 * KEY_WIDTH)), axis=0)
    plane_kv = kv_slots.reshape(shards * rows_here, 2 * KEY_WIDTH)
    window_part = to_low(dot(window_pick, plane_kv)).reshape(planes, sequences, window_rows, 2 * KEY_WIDTH)
    window_here = line.scatter([window_part[r] for r in range(planes)])
    pw_slots = jnp.concatenate(over_fsdp.pieces(window_here), axis=0)
    kv_slots = kv_slots.reshape(shards, sequences, positions, 2 * KEY_WIDTH)
    pw_slots = pw_slots.reshape(shards, sequences, window_rows, 2 * KEY_WIDTH)
    attended_b = attend_fwd(meta, query_b, kv_slots, pw_slots, dims)
    attn_proj = dot_t(attended_b, out_w)
    laurel_mid_b = to_low(dot(hidden_b, laurel_w[:, :RESIDUAL_RANK]))
    laurel_back = dot_t(laurel_mid_b, laurel_w[:, RESIDUAL_RANK:])
    first_sum = combine(x_float, attn_proj, laurel_back, hidden, scales[1], scales[2])
    ffn_in_b = to_low(rms_norm(first_sum, scales[3]))

    cot_float = cotangent.reshape(rows_here, model_width).astype(F32) * live
    chunks = []
    for i in range(sequences):
        rows = slice(i * positions, (i + 1) * positions)
        with jax.named_scope("gather_in_%d" % i):
            pieces = over_fsdp.pieces(ffn_in_b[rows])
        with jax.named_scope("ffn_fwd_%d" % i):
            (act_b, slope_b, value_b), ffn_in, parts = ffn_fwd(pieces, ffn_w, spans)
        with jax.named_scope("scatter_out_%d" % i):
            down_vals = over_fsdp.scatter(parts).astype(F32)
        second_sum = residual_norm(first_sum[rows], down_vals, scales[4])
        second_b = to_low(second_sum)
        layer_gate = dot(second_b, layer_w[:, :PER_LAYER_WIDTH])
        layer_mix_b = to_low(gated(layer_gate, layer_float[rows]))
        layer_back = dot_t(layer_mix_b, layer_w[:, PER_LAYER_WIDTH:])
        output, pull_out = jax.vjp(residual_norm, second_sum, layer_back, scales[5])
        mixed = to_low(output * live[rows])
        grad_second, grad_layer_back, gain_five = pull_out(cot_float[rows])
        grad_back_b = to_low(grad_layer_back)
        grad_mix = to_low(dot(grad_back_b, layer_w[:, PER_LAYER_WIDTH:])).astype(F32)
        unused_act, pull_act = jax.vjp(gated, layer_gate, layer_float[rows])
        grad_gate_layer, grad_layer_in = pull_act(grad_mix)
        grad_gate_b = to_low(grad_gate_layer)
        grad_second = grad_second + dot_t(grad_gate_b, layer_w[:, :PER_LAYER_WIDTH])
        unused_mid, pull_mid = jax.vjp(residual_norm, first_sum[rows], down_vals, scales[4])
        grad_first, grad_down, gain_four = pull_mid(grad_second)
        with jax.named_scope("gather_grad_%d" % i):
            pieces = over_fsdp.pieces(to_low(grad_down))
        with jax.named_scope("ffn_bwd_%d" % i):
            grad_gate_h, grad_up_h, grad_down_all, parts = ffn_bwd(pieces, ffn_w, slope_b, value_b, spans)
        with jax.named_scope("scatter_grad_%d" % i):
            grad_ffn_in = over_fsdp.scatter(parts).astype(F32)
        unused_pre, pull_pre = jax.vjp(rms_norm, first_sum[rows], scales[3])
        grad_first_b, gain_three = pull_pre(grad_ffn_in)
        chunks.append(
            dict(
                mixed=mixed,
                grad_layer_in=to_low(grad_layer_in),
                grad_first=grad_first + grad_first_b,
                ffn_in=ffn_in,
                act=act_b,
                grad_down=grad_down_all,
                grad_gate=grad_gate_h,
                grad_up=grad_up_h,
                second=second_b,
                grad_gate_layer=grad_gate_b,
                grad_back=grad_back_b,
                layer_mix=layer_mix_b,
                gains=(gain_three, gain_four, gain_five),
            )
        )

    def joined(name):
        return jnp.concatenate([c[name] for c in chunks], axis=0)

    def listed(name):
        return [c[name] for c in chunks]

    plane_slot = (jnp.arange(planes, dtype=jnp.int32) - plane) % planes
    row_part = width_here // planes

    def to_owners(parts, name):
        with jax.named_scope("sum_" + name):
            mine = line.scatter([parts[r] for r in range(planes)])
        with jax.named_scope("deal_" + name):
            theirs = lax.all_to_all(mine, "fsdp", split_axis=0, concat_axis=0, tiled=True)
        with jax.named_scope("spread_" + name):
            return line.gather(theirs)

    def placed(all_kinds):
        width = len(all_kinds) * HIDDEN_UNITS
        whole = jnp.zeros((width_here, width), F32)
        for r in range(planes):
            rows = jnp.concatenate(
                [jnp.swapaxes(kind[r], 0, 1).reshape(row_part, HIDDEN_UNITS) for kind in all_kinds], axis=1
            ).astype(F32)
            whole = lax.dynamic_update_slice(whole, rows, (((plane + r) % planes) * row_part, 0))
        return whole

    with jax.named_scope("down_grad"):
        (down_parts,) = rows_grad(plane_slot, listed("grad_down"), [listed("act")], planes, shards)
    with jax.named_scope("gate_up_grad"):
        gate_parts, up_parts = rows_grad(
            plane_slot, listed("ffn_in"), [listed("grad_gate"), listed("grad_up")], planes, shards
        )
    ffn_down_grad = placed([to_owners(down_parts, "down")])
    gate_rows = to_owners(gate_parts, "gate")
    up_rows = to_owners(up_parts, "up")
    gate_up_grad = placed([gate_rows, up_rows])

    grad_first = joined("grad_first")
    unused_comb, pull_combine = jax.vjp(
        combine, x_float, attn_proj, laurel_back, hidden, scales[1], scales[2]
    )
    grad_x_one, grad_proj, grad_laurel, grad_hidden, gain_one, gain_two = pull_combine(grad_first)
    grad_proj_b = to_low(grad_proj)
    grad_laurel_b = to_low(grad_laurel)
    grad_mid_b = to_low(dot(grad_laurel_b, laurel_w[:, RESIDUAL_RANK:]))
    grad_attended_b = to_low(dot(grad_proj_b, out_w))
    with jax.named_scope("small_grad"):
        joined_mid = jnp.concatenate([grad_mid_b, jnp.zeros_like(grad_mid_b)], axis=1)
        mid_joined = jnp.concatenate([jnp.zeros_like(laurel_mid_b), laurel_mid_b], axis=1)
        small_parts = owner_grad(
            fsdp_sources,
            [grad_proj_b, hidden_b, grad_laurel_b, joined("second"), joined("grad_back")],
            [attended_b, joined_mid, mid_joined, joined("grad_gate_layer"), joined("layer_mix")],
            [False, False, True, False, False],
            spans,
        )
    with jax.named_scope("attend_bwd"):
        grad_query, gkv_part, gpw_part = attend_bwd(meta, query_b, kv_slots, pw_slots, grad_attended_b, dims)
    grad_q_b, grad_q_head = heads_bwd(
        qkv, 0, QUERY_HEADS, QUERY_HEADS, cosine, sine, head_scales[0:1], grad_query, positions
    )
    with jax.named_scope("query_grad"):
        query_parts = owner_grad(fsdp_sources, [hidden_b], [grad_q_b], [False], spans)
    with jax.named_scope("window_back"):
        gpw_here = over_fsdp.scatter_whole(gpw_part.reshape(shards * sequences, window_rows, 2 * KEY_WIDTH))
        gpw_all = jnp.concatenate(line.gather(gpw_here), axis=0).reshape(-1, 2 * KEY_WIDTH)
    gkv_sum = t_dot(window_pick, gpw_all) + gkv_part.reshape(-1, 2 * KEY_WIDTH).astype(F32)
    with jax.named_scope("keys_back"):
        grad_kv = over_fsdp.scatter_whole(
            to_low(gkv_sum).reshape(shards * sequences, positions, 2 * KEY_WIDTH)
        ).reshape(rows_here, 2 * KEY_WIDTH)
    grad_kv_b, grad_k_head = heads_bwd(
        qkv, QUERY_HEADS, 2 * KEY_VALUE_HEADS, KEY_VALUE_HEADS, cosine, sine, head_scales[1:2], grad_kv, positions
    )
    with jax.named_scope("keys_grad"):
        keys_parts = owner_grad(fsdp_sources, [hidden_b], [grad_kv_b], [False], spans)
    grad_hidden = (
        grad_hidden
        + dot_t(grad_mid_b, laurel_w[:, :RESIDUAL_RANK])
        + dot_t(grad_q_b, in_w[:, :QUERY_WIDTH])
        + dot_t(grad_kv_b, in_w[:, QUERY_WIDTH:])
    )
    unused_norm, pull_in = jax.vjp(rms_norm, x_float, scales[0])
    grad_x_two, gain_zero = pull_in(grad_hidden)
    input_grad = to_low(grad_x_one + grad_x_two).reshape(tokens.shape)

    def owned(parts, name):
        with jax.named_scope("own_" + name):
            mine = over_fsdp.scatter(parts)[0]
            quarters = mine.reshape(planes, row_part, mine.shape[1])
            ordered = [lax.dynamic_index_in_dim(quarters, plane_order[r], 0, keepdims=False) for r in range(planes)]
        with jax.named_scope("all_" + name):
            return line.gather(line.scatter(ordered))

    def stacked(rows):
        whole = jnp.zeros((width_here, rows[0].shape[1]), F32)
        for r in range(planes):
            whole = lax.dynamic_update_slice(whole, rows[r].astype(F32), (plane_order[r] * row_part, 0))
        return whole

    small_grad = stacked(owned(small_parts, "small"))
    query_rows = owned(query_parts, "query")
    keys_rows = owned(keys_parts, "keys")
    attn_in_grad = stacked([jnp.concatenate([q, k], axis=1) for q, k in zip(query_rows, keys_rows)])

    gain_rows = jnp.stack(
        [gain_zero, gain_one, gain_two] + [sum(c["gains"][k] for c in chunks) for k in range(3)]
    )
    grad_head = jnp.concatenate([grad_q_head, grad_k_head], axis=0)
    packed = jnp.concatenate([gain_rows, jnp.pad(grad_head, ((0, 0), (0, model_width - HEAD_DIM)))], axis=0)
    packed = over_rep.total(over_fsdp.total(packed))
    gain_share = lax.dynamic_slice_in_dim(packed[:6], shard * width_here, width_here, 1)
    return (
        jnp.stack([c["mixed"] for c in chunks]),
        input_grad,
        jnp.stack([c["grad_layer_in"] for c in chunks]),
        attn_in_grad,
        small_grad[:, :QUERY_WIDTH],
        gate_up_grad,
        ffn_down_grad,
        small_grad[:, QUERY_WIDTH : QUERY_WIDTH + 2 * RESIDUAL_RANK],
        small_grad[:, QUERY_WIDTH + 2 * RESIDUAL_RANK :],
        gain_share,
        packed[6:8, :HEAD_DIM],
    )


def solution(mesh):
    rows = P("rep", "fsdp", None)
    weight = P("fsdp", None)
    return jax.shard_map(
        on_device,
        mesh=mesh,
        in_specs=(rows, rows, rows, P(), P()) + (weight,) * 6 + (P(None, "fsdp"), P()),
        out_specs=(rows, rows, rows) + (weight,) * 6 + (P(None, "fsdp"), P()),
        check_vma=False,
    )
```

```python
import jax
import jax.numpy as jnp
import numpy as np
from jax import lax
from jax.experimental import pallas as pl
from jax.experimental.pallas import tpu as pltpu
from jax.sharding import PartitionSpec as P

QUERY_HEADS = 8
KEY_VALUE_HEADS = 2
HEADS_PER_KEY = QUERY_HEADS // KEY_VALUE_HEADS
HEAD_DIM = 256
HALF_DIM = HEAD_DIM // 2
HIDDEN_UNITS = 8192
RESIDUAL_RANK = 64
PER_LAYER_WIDTH = 256
WINDOW = 512
QUERY_WIDTH = QUERY_HEADS * HEAD_DIM
KEY_WIDTH = KEY_VALUE_HEADS * HEAD_DIM

EPS = 1e-06
BASE = 10000.0
ROOT_HALF = 0.7071067811865476
NEG_FILL = -1e30
SCALE = HEAD_DIM ** (-0.5)

F32 = jnp.float32
BF16 = jnp.bfloat16


def rms_norm(values, scales):
    return values * lax.rsqrt(jnp.mean(values * values, axis=-1, keepdims=True) + EPS) * scales


def gelu_tanh(values):
    return jax.nn.gelu(values, approximate=True)


def frequencies():
    return 1.0 / BASE ** (jnp.arange(HALF_DIM, dtype=F32) * 2.0 / HEAD_DIM)


def combine(x_float, attn_proj, laurel_back, hidden, scale_one, scale_two):
    return (
        x_float + rms_norm(attn_proj, scale_two) + hidden + rms_norm(laurel_back, scale_one)
    ) * ROOT_HALF


def gated(gate, up):
    return gelu_tanh(gate) * up


def residual_norm(base, values, scales):
    return base + rms_norm(values, scales)


def to_low(values):
    return values.astype(BF16)


def dot(left, right):
    return jnp.dot(left, right, preferred_element_type=F32)


def dot_t(left, right):
    return lax.dot_general(left, right, (((1,), (1,)), ((), ())), preferred_element_type=F32)


def t_dot(left, right):
    return lax.dot_general(left, right, (((0,), (0,)), ((), ())), preferred_element_type=F32)


def fsdp_phases(count):
    bits = [1 << k for k in range(1, count.bit_length() - 1)]
    phases = []
    for k in range(len(bits)):
        phases.append([i ^ (bits[k] if i % 2 == 0 else bits[len(bits) - 1 - k]) for i in range(count)])
    phases.append([i ^ 1 for i in range(count)])
    return phases


def rep_phases(count):
    bits = [1 << k for k in range(count.bit_length() - 1)]
    return [[i ^ b for i in range(count)] for b in reversed(bits)]


def slot_table(phases, count):
    held = [[i] for i in range(count)]
    for perm in phases:
        held = [held[i] + held[perm[i]] for i in range(count)]
    return np.array(held, dtype=np.int32).T


class Exchange:
    def __init__(self, axis, phases, count):
        self.axis = axis
        self.count = count
        self.perms = [[(i, p[i]) for i in range(count)] for p in phases]
        self.table = slot_table(phases, count)
        inverse = np.zeros_like(self.table)
        for i in range(count):
            inverse[self.table[:, i], i] = np.arange(count)
        self.inverse = inverse

    def sources(self, index):
        return lax.dynamic_index_in_dim(jnp.asarray(self.table), index, 1, keepdims=False)

    def slots(self, index):
        return lax.dynamic_index_in_dim(jnp.asarray(self.inverse), index, 1, keepdims=False)

    def pieces(self, piece):
        held = [piece]
        for perm in self.perms:
            held = held + [lax.ppermute(h, self.axis, perm) for h in held]
        return held

    def groups(self):
        return [(0, 1)] + [(1 << k, 2 << k) for k in range(len(self.perms))]

    def scatter(self, parts):
        spans = self.groups()
        for k in range(len(self.perms), 0, -1):
            got = lax.ppermute(parts[k], self.axis, self.perms[k - 1])
            step = got.shape[0] // spans[k][0]
            parts = [
                (parts[j].astype(F32) + got[spans[j][0] * step : spans[j][1] * step].astype(F32)).astype(got.dtype)
                for j in range(k)
            ]
        return parts[0]

    def scatter_whole(self, whole):
        step = whole.shape[0] // self.count
        return self.scatter([whole[lo * step : hi * step] for lo, hi in self.groups()])

    def total(self, value):
        for perm in self.perms:
            value = value + lax.ppermute(value, self.axis, perm)
        return value


def heads_fwd_body(qkv_ref, cos_ref, sin_ref, gains_ref, q_ref, kv_ref):
    cosine = cos_ref[...]
    sine = sin_ref[...]
    for c in range(QUERY_HEADS + 2 * KEY_VALUE_HEADS):
        head = qkv_ref[:, c * HEAD_DIM : (c + 1) * HEAD_DIM]
        normed = head * lax.rsqrt(jnp.mean(head * head, axis=-1, keepdims=True) + EPS)
        if c < QUERY_HEADS + KEY_VALUE_HEADS:
            row = 0 if c < QUERY_HEADS else 1
            normed = normed * gains_ref[row : row + 1, :]
            low = normed[:, :HALF_DIM]
            high = normed[:, HALF_DIM:]
            first = to_low(low * cosine - high * sine)
            second = to_low(high * cosine + low * sine)
        else:
            first = to_low(normed[:, :HALF_DIM])
            second = to_low(normed[:, HALF_DIM:])
        if c < QUERY_HEADS:
            q_ref[:, c * HEAD_DIM : c * HEAD_DIM + HALF_DIM] = first
            q_ref[:, c * HEAD_DIM + HALF_DIM : (c + 1) * HEAD_DIM] = second
        else:
            at = (c - QUERY_HEADS) * HEAD_DIM
            kv_ref[:, at : at + HALF_DIM] = first
            kv_ref[:, at + HALF_DIM : at + HEAD_DIM] = second


def heads_fwd(qkv, cosine, sine, head_scales, block):
    rows, width = qkv.shape
    return pl.pallas_call(
        heads_fwd_body,
        grid=(rows // block,),
        in_specs=[
            pl.BlockSpec((block, width), lambda i: (i, 0)),
            pl.BlockSpec((block, HALF_DIM), lambda i: (i, 0)),
            pl.BlockSpec((block, HALF_DIM), lambda i: (i, 0)),
            pl.BlockSpec((2, HEAD_DIM), lambda i: (0, 0)),
        ],
        out_specs=[
            pl.BlockSpec((block, QUERY_WIDTH), lambda i: (i, 0)),
            pl.BlockSpec((block, 2 * KEY_WIDTH), lambda i: (i, 0)),
        ],
        out_shape=[
            jax.ShapeDtypeStruct((rows, QUERY_WIDTH), BF16),
            jax.ShapeDtypeStruct((rows, 2 * KEY_WIDTH), BF16),
        ],
        name="heads_fwd",
    )(qkv, cosine, sine, head_scales)


def heads_bwd_body(heads, gained, qkv_ref, cos_ref, sin_ref, gains_ref, grad_ref, out_ref, gain_ref):
    @pl.when(pl.program_id(0) == 0)
    def _():
        gain_ref[...] = jnp.zeros_like(gain_ref)

    cosine = cos_ref[...]
    sine = sin_ref[...]
    total = jnp.zeros((1, HEAD_DIM), F32)
    for c in range(heads):
        here = slice(c * HEAD_DIM, (c + 1) * HEAD_DIM)
        head = qkv_ref[:, here]
        scale = lax.rsqrt(jnp.mean(head * head, axis=-1, keepdims=True) + EPS)
        normed = head * scale
        grad = grad_ref[:, here].astype(F32)
        if c < gained:
            first = grad[:, :HALF_DIM]
            second = grad[:, HALF_DIM:]
            grad = jnp.concatenate(
                [first * cosine + second * sine, second * cosine - first * sine], axis=1
            )
            total = total + jnp.sum(grad * normed, axis=0, keepdims=True)
            grad = grad * gains_ref[...]
        back = scale * (grad - normed * jnp.mean(grad * normed, axis=-1, keepdims=True))
        out_ref[:, here] = to_low(back)
    gain_ref[...] += total


def heads_bwd(qkv, first, heads, gained, cosine, sine, head_scale, grad, block):
    rows = qkv.shape[0]
    width = heads * HEAD_DIM
    at = first // heads
    return pl.pallas_call(
        lambda *refs: heads_bwd_body(heads, gained, *refs),
        grid=(rows // block,),
        in_specs=[
            pl.BlockSpec((block, width), lambda i: (i, at)),
            pl.BlockSpec((block, HALF_DIM), lambda i: (i, 0)),
            pl.BlockSpec((block, HALF_DIM), lambda i: (i, 0)),
            pl.BlockSpec((1, HEAD_DIM), lambda i: (0, 0)),
            pl.BlockSpec((block, width), lambda i: (i, 0)),
        ],
        out_specs=[
            pl.BlockSpec((block, width), lambda i: (i, 0)),
            pl.BlockSpec((1, HEAD_DIM), lambda i: (0, 0)),
        ],
        out_shape=[
            jax.ShapeDtypeStruct((rows, width), BF16),
            jax.ShapeDtypeStruct((1, HEAD_DIM), F32),
        ],
        name="heads_bwd",
    )(qkv, cosine, sine, head_scale, grad)


def load_window(meta_ref, kv_ref, pw_ref, keys_ref, sequences, positions, window_rows, shards):
    blocks = WINDOW // positions + 1
    per_block = positions // window_rows
    for b in range(blocks):
        slot = meta_ref[sequences + b]

        @pl.when(slot >= 0)
        def _():
            keys_ref[b * positions : (b + 1) * positions, :] = kv_ref[jnp.maximum(slot, 0), 0]

        @pl.when(slot < 0)
        def _():
            for m in range(per_block):
                piece = meta_ref[sequences + blocks + b * per_block + m]
                at = b * positions + m * window_rows
                keys_ref[at : at + window_rows, :] = pw_ref[piece, 0]


def window_mask(meta_ref, positions):
    width = WINDOW + positions
    row = lax.broadcasted_iota(jnp.int32, (positions, width), 0)
    col = lax.broadcasted_iota(jnp.int32, (positions, width), 1)
    low = meta_ref[pl.program_id(0)]
    return (col > row) & (col <= row + WINDOW) & (col >= low)


def head_probs(query, keys, allowed):
    scores = dot_t(query, keys) * SCALE
    masked = jnp.where(allowed, scores, NEG_FILL)
    top = jnp.max(masked, axis=-1, keepdims=True)
    powers = jnp.exp(masked - top)
    return powers / jnp.sum(powers, axis=-1, keepdims=True)


def attend_fwd_body(sequences, positions, window_rows, shards, meta_ref, q_ref, kv_ref, pw_ref, o_ref, keys_ref):
    load_window(meta_ref, kv_ref, pw_ref, keys_ref, sequences, positions, window_rows, shards)
    allowed = window_mask(meta_ref, positions)
    for a in range(KEY_VALUE_HEADS):
        keys = keys_ref[:, a * HEAD_DIM : (a + 1) * HEAD_DIM]
        vals = keys_ref[:, KEY_WIDTH + a * HEAD_DIM : KEY_WIDTH + (a + 1) * HEAD_DIM]
        for g in range(HEADS_PER_KEY):
            c = a * HEADS_PER_KEY + g
            probs = head_probs(q_ref[:, c * HEAD_DIM : (c + 1) * HEAD_DIM], keys, allowed)
            o_ref[:, c * HEAD_DIM : (c + 1) * HEAD_DIM] = to_low(dot(to_low(probs), vals))


def attend_bwd_body(
    sequences, positions, window_rows, shards,
    meta_ref, q_ref, kv_ref, pw_ref, go_ref, gq_ref, gkv_ref, gpw_ref, keys_ref, grads_ref,
):
    load_window(meta_ref, kv_ref, pw_ref, keys_ref, sequences, positions, window_rows, shards)
    allowed = window_mask(meta_ref, positions)
    for a in range(KEY_VALUE_HEADS):
        keys = keys_ref[:, a * HEAD_DIM : (a + 1) * HEAD_DIM]
        vals = keys_ref[:, KEY_WIDTH + a * HEAD_DIM : KEY_WIDTH + (a + 1) * HEAD_DIM]
        grad_keys = jnp.zeros((WINDOW + positions, HEAD_DIM), F32)
        grad_vals = jnp.zeros((WINDOW + positions, HEAD_DIM), F32)
        for g in range(HEADS_PER_KEY):
            c = a * HEADS_PER_KEY + g
            query = q_ref[:, c * HEAD_DIM : (c + 1) * HEAD_DIM]
            grad_out = go_ref[:, c * HEAD_DIM : (c + 1) * HEAD_DIM]
            probs = head_probs(query, keys, allowed)
            grad_probs = dot_t(grad_out, vals)
            delta = jnp.sum(probs * grad_probs, axis=-1, keepdims=True)
            grad_scores = to_low(probs * (grad_probs - delta))
            gq_ref[:, c * HEAD_DIM : (c + 1) * HEAD_DIM] = dot(grad_scores, keys) * SCALE
            grad_keys = grad_keys + t_dot(grad_scores, query)
            grad_vals = grad_vals + t_dot(to_low(probs), grad_out)
        grads_ref[:, a * HEAD_DIM : (a + 1) * HEAD_DIM] = to_low(grad_keys * SCALE)
        grads_ref[:, KEY_WIDTH + a * HEAD_DIM : KEY_WIDTH + (a + 1) * HEAD_DIM] = to_low(grad_vals)
    gkv_ref[...] = jnp.zeros_like(gkv_ref)
    gpw_ref[...] = jnp.zeros_like(gpw_ref)
    blocks = WINDOW // positions + 1
    per_block = positions // window_rows
    for b in range(blocks):
        slot = meta_ref[sequences + b]

        @pl.when(slot >= 0)
        def _():
            gkv_ref[jnp.maximum(slot, 0), 0] = grads_ref[b * positions : (b + 1) * positions, :]

        @pl.when(slot < 0)
        def _():
            for m in range(per_block):
                piece = meta_ref[sequences + blocks + b * per_block + m]
                at = b * positions + m * window_rows
                gpw_ref[piece, 0] = grads_ref[at : at + window_rows, :]


def attention_specs(sequences, positions, window_rows, shards):
    rows = pl.BlockSpec((positions, QUERY_WIDTH), lambda i, m: (i, 0))
    kv = pl.BlockSpec((shards, 1, positions, 2 * KEY_WIDTH), lambda i, m: (0, i, 0, 0))
    pw = pl.BlockSpec((shards, 1, window_rows, 2 * KEY_WIDTH), lambda i, m: (0, i, 0, 0))
    return rows, kv, pw


def attend_fwd(meta, query, kv_slots, pw_slots, dims):
    sequences, positions, window_rows, shards = dims
    rows, kv, pw = attention_specs(*dims)
    return pl.pallas_call(
        lambda *refs: attend_fwd_body(*dims, *refs),
        grid_spec=pltpu.PrefetchScalarGridSpec(
            num_scalar_prefetch=1,
            grid=(sequences,),
            in_specs=[rows, kv, pw],
            out_specs=rows,
            scratch_shapes=[pltpu.VMEM((WINDOW + positions, 2 * KEY_WIDTH), BF16)],
        ),
        out_shape=jax.ShapeDtypeStruct((sequences * positions, QUERY_WIDTH), BF16),
        name="attend_fwd",
    )(meta, query, kv_slots, pw_slots)


def attend_bwd(meta, query, kv_slots, pw_slots, grad_out, dims):
    sequences, positions, window_rows, shards = dims
    rows, kv, pw = attention_specs(*dims)
    return pl.pallas_call(
        lambda *refs: attend_bwd_body(*dims, *refs),
        grid_spec=pltpu.PrefetchScalarGridSpec(
            num_scalar_prefetch=1,
            grid=(sequences,),
            in_specs=[rows, kv, pw, rows],
            out_specs=[rows, kv, pw],
            scratch_shapes=[
                pltpu.VMEM((WINDOW + positions, 2 * KEY_WIDTH), BF16),
                pltpu.VMEM((WINDOW + positions, 2 * KEY_WIDTH), BF16),
            ],
        ),
        out_shape=[
            jax.ShapeDtypeStruct((sequences * positions, QUERY_WIDTH), F32),
            jax.ShapeDtypeStruct(kv_slots.shape, BF16),
            jax.ShapeDtypeStruct(pw_slots.shape, BF16),
        ],
        name="attend_bwd",
    )(meta, query, kv_slots, pw_slots, grad_out)


GELU_A = 0.7978845608028654
GELU_B = 0.044715


def take_slots(refs, all_ref, step, rows):
    each = all_ref.shape[0] // rows
    for k, ref in enumerate(refs):

        @pl.when(step == k // each)
        def _():
            at = (k % each) * rows
            all_ref[at : at + rows, :] = ref[...]


def give_slots(result, spans, out_refs, step, rows):
    each = result.shape[0] // rows
    for (lo, hi), ref in zip(spans, out_refs):
        for k in range(lo, hi):

            @pl.when(step == k // each)
            def _():
                at = (k % each) * rows
                ref[(k - lo) * rows : (k - lo + 1) * rows, :] = result[at : at + rows, :]


def ffn_fwd_body(shards, spans, *refs):
    x_refs = refs[:shards]
    w_ref = refs[shards]
    act_ref, slope_ref, value_ref, all_ref = refs[shards + 1 : shards + 5]
    out_refs = refs[shards + 5 :]
    rows = x_refs[0].shape[0]
    hidden = w_ref.shape[1] // 3
    step = pl.program_id(0)
    take_slots(x_refs, all_ref, step, rows)
    inputs = all_ref[...]
    gate = dot(inputs, w_ref[:, :hidden])
    up = dot(inputs, w_ref[:, hidden : 2 * hidden])
    squared = gate * gate
    bend = jnp.tanh(GELU_A * gate * (1.0 + GELU_B * squared))
    half = 0.5 * (1.0 + bend)
    value = gate * half
    slope = half + (0.5 * GELU_A) * gate * (1.0 - bend * bend) * (1.0 + 3.0 * GELU_B * squared)
    act = to_low(value * up)
    act_ref[...] = act
    slope_ref[...] = to_low(slope * up)
    value_ref[...] = to_low(value)
    give_slots(to_low(dot_t(act, w_ref[:, 2 * hidden :])), spans, out_refs, step, rows)


def ffn_specs(shards, rows, width, hidden, spans):
    every = shards * rows
    block = min(256, every)
    row = lambda n: pl.BlockSpec((block, n), lambda j: (j, 0))
    pieces = [pl.BlockSpec((rows, width), lambda j: (0, 0))] * shards
    weights = pl.BlockSpec((width, 3 * hidden), lambda j: (0, 0), pipeline_mode=pl.Buffered(1))
    groups = [pl.BlockSpec(((hi - lo) * rows, width), lambda j: (0, 0)) for lo, hi in spans]
    shapes = [jax.ShapeDtypeStruct(((hi - lo) * rows, width), BF16) for lo, hi in spans]
    return every, every // block, row, pieces, weights, groups, shapes


def ffn_fwd(pieces, weights, spans):
    shards = len(pieces)
    rows, width = pieces[0].shape
    hidden = weights.shape[1] // 3
    every, steps, row, piece_specs, weight_spec, groups, group_shapes = ffn_specs(shards, rows, width, hidden, spans)
    outs = pl.pallas_call(
        lambda *refs: ffn_fwd_body(shards, spans, *refs),
        grid=(steps,),
        in_specs=piece_specs + [weight_spec],
        out_specs=[row(hidden)] * 3 + [row(width)] + groups,
        out_shape=[jax.ShapeDtypeStruct((every, hidden), BF16)] * 3
        + [jax.ShapeDtypeStruct((every, width), BF16)]
        + group_shapes,
        compiler_params=pltpu.CompilerParams(vmem_limit_bytes=60 << 20),
        cost_estimate=pl.CostEstimate(
            flops=6 * every * width * hidden, transcendentals=every * hidden,
            bytes_accessed=2 * (3 * width * hidden + 3 * every * width + 3 * every * hidden),
        ),
        name="ffn_fwd",
    )(*pieces, weights)
    return outs[:3], outs[3], outs[4:]


def ffn_bwd_body(shards, spans, *refs):
    g_refs = refs[:shards]
    w_ref, slope_ref, value_ref = refs[shards : shards + 3]
    gg_ref, gu_ref, all_ref = refs[shards + 3 : shards + 6]
    out_refs = refs[shards + 6 :]
    rows = g_refs[0].shape[0]
    hidden = w_ref.shape[1] // 3
    step = pl.program_id(0)
    take_slots(g_refs, all_ref, step, rows)
    grad = to_low(dot(all_ref[...], w_ref[:, 2 * hidden :])).astype(F32)
    grad_gate = to_low(grad * slope_ref[...].astype(F32))
    grad_up = to_low(grad * value_ref[...].astype(F32))
    gg_ref[...] = grad_gate
    gu_ref[...] = grad_up
    back = dot_t(grad_gate, w_ref[:, :hidden]) + dot_t(grad_up, w_ref[:, hidden : 2 * hidden])
    give_slots(to_low(back), spans, out_refs, step, rows)


def ffn_bwd(pieces, weights, slope, value, spans):
    shards = len(pieces)
    rows, width = pieces[0].shape
    hidden = weights.shape[1] // 3
    every, steps, row, piece_specs, weight_spec, groups, group_shapes = ffn_specs(shards, rows, width, hidden, spans)
    outs = pl.pallas_call(
        lambda *refs: ffn_bwd_body(shards, spans, *refs),
        grid=(steps,),
        in_specs=piece_specs + [weight_spec] + [row(hidden)] * 2,
        out_specs=[row(hidden)] * 2 + [row(width)] + groups,
        out_shape=[jax.ShapeDtypeStruct((every, hidden), BF16)] * 2
        + [jax.ShapeDtypeStruct((every, width), BF16)]
        + group_shapes,
        compiler_params=pltpu.CompilerParams(vmem_limit_bytes=60 << 20),
        cost_estimate=pl.CostEstimate(
            flops=6 * every * width * hidden, transcendentals=0,
            bytes_accessed=2 * (3 * width * hidden + 3 * every * width + 4 * every * hidden),
        ),
        name="ffn_bwd",
    )(*pieces, weights, slope, value)
    return outs[0], outs[1], outs[2], outs[3:]


def rows_grad_body(planes, count, kinds, *refs):
    lefts = refs[:count]
    rights = refs[count : count + count * kinds]
    out = refs[-1]
    for k in range(kinds):
        total = t_dot(lefts[0][...], rights[k * count][...])
        for c in range(1, count):
            total = total + t_dot(lefts[c][...], rights[k * count + c][...])
        total = to_low(total)
        rows, hidden = total.shape[0] // planes, total.shape[1]
        for q in range(planes):
            out[q, 0, :, k * hidden : (k + 1) * hidden] = total[q * rows : (q + 1) * rows, :]


def rows_grad(lefts, kinds, planes, shards):
    count = len(lefts)
    rows, width = lefts[0].shape
    block = width // shards
    flat = [r for rights in kinds for r in rights]
    hidden = flat[0].shape[1]
    part = block // planes
    wide = len(kinds) * hidden
    return pl.pallas_call(
        lambda *refs: rows_grad_body(planes, count, len(kinds), *refs),
        grid=(shards,),
        in_specs=[pl.BlockSpec((rows, block), lambda f: (0, f))] * count
        + [pl.BlockSpec((rows, hidden), lambda f: (0, 0), pipeline_mode=pl.Buffered(1))] * len(flat),
        out_specs=pl.BlockSpec((planes, 1, part, wide), lambda f: (0, f, 0, 0)),
        out_shape=jax.ShapeDtypeStruct((planes, shards, part, wide), BF16),
        compiler_params=pltpu.CompilerParams(vmem_limit_bytes=60 << 20),
        cost_estimate=pl.CostEstimate(
            flops=2 * count * rows * width * wide, transcendentals=0,
            bytes_accessed=2 * (count * rows * width + len(flat) * rows * hidden + width * wide),
        ),
        name="rows_grad",
    )(*lefts, *flat)


def owner_grad_body(pairs, spans, order_ref, *refs):
    lefts = refs[: len(pairs)]
    rights = refs[len(pairs) : 2 * len(pairs)]
    outs = refs[2 * len(pairs) :]
    step = pl.program_id(0)
    for ref, (lo, hi) in zip(outs, spans):

        @pl.when((step >= lo) & (step < hi))
        def _():
            at = 0
            parts = []
            for n, (left, right) in enumerate(zip(lefts, rights)):
                value = t_dot(left[...], right[...])
                if pairs[n]:
                    parts[-1] = parts[-1] + value
                else:
                    parts.append(value)
            for value in parts:
                ref[0, :, at : at + value.shape[1]] = to_low(value)
                at += value.shape[1]


def owner_grad(order, lefts, rights, joins, spans):
    shards = spans[-1][1]
    rows, width = lefts[0].shape
    block = width // shards
    total = sum(r.shape[1] for r, j in zip(rights, joins) if not j)
    return pl.pallas_call(
        lambda *refs: owner_grad_body(joins, spans, *refs),
        grid_spec=pltpu.PrefetchScalarGridSpec(
            num_scalar_prefetch=1,
            grid=(shards,),
            in_specs=[pl.BlockSpec((rows, block), lambda t, o: (0, o[t]))] * len(lefts)
            + [pl.BlockSpec(r.shape, lambda t, o: (0, 0)) for r in rights],
            out_specs=[
                pl.BlockSpec((1, block, total), lambda t, o, lo=lo, hi=hi: (jnp.clip(t - lo, 0, hi - lo - 1), 0, 0))
                for lo, hi in spans
            ],
        ),
        out_shape=[jax.ShapeDtypeStruct((hi - lo, block, total), BF16) for lo, hi in spans],
        compiler_params=pltpu.CompilerParams(vmem_limit_bytes=60 << 20),
        cost_estimate=pl.CostEstimate(
            flops=2 * rows * width * sum(r.shape[1] for r in rights), transcendentals=0,
            bytes_accessed=2 * (rows * width * len(lefts) + rows * total + width * total),
        ),
        name="owner_grad",
    )(order, *lefts, *rights)


def on_device(
    tokens,
    layer_input,
    cotangent,
    lengths,
    deal_order,
    attention_input_weight,
    attn_out,
    gate_up,
    ffn_down,
    laurel_pair,
    layer_pair,
    norm_gains,
    head_gains,
):
    sequences, positions, model_width = tokens.shape
    plane = lax.axis_index("rep")
    shard = lax.axis_index("fsdp")
    planes = lax.axis_size("rep")
    shards = lax.axis_size("fsdp")
    rows_here = sequences * positions
    window_rows = WINDOW // shards
    width_here = model_width // shards
    dims = (sequences, positions, window_rows, shards)
    over_fsdp = Exchange("fsdp", fsdp_phases(shards), shards)
    over_rep = Exchange("rep", rep_phases(planes), planes)

    spans = over_fsdp.groups()
    hidden_here = HIDDEN_UNITS // shards

    with jax.named_scope("gather_in"):
        in_w = lax.all_gather(attention_input_weight, "fsdp", axis=0, tiled=True)

    def by_owner(part):
        return jnp.swapaxes(part.reshape(width_here, shards, hidden_here), 0, 1)

    send = lax.optimization_barrier(
        jnp.concatenate(
            [by_owner(gate_up[:, :HIDDEN_UNITS]), by_owner(gate_up[:, HIDDEN_UNITS:]), by_owner(ffn_down)], axis=2
        )
    )
    with jax.named_scope("deal_ffn"):
        ffn_w = lax.all_to_all(send, "fsdp", split_axis=0, concat_axis=0, tiled=True)
    ffn_w = ffn_w.reshape(model_width, 3 * hidden_here)
    small = jnp.concatenate([attn_out, laurel_pair, layer_pair], axis=1)
    with jax.named_scope("gather_small"):
        small_w = lax.all_gather(small, "fsdp", axis=0, tiled=True)
    out_w = small_w[:, :QUERY_WIDTH]
    laurel_w = small_w[:, QUERY_WIDTH : QUERY_WIDTH + 2 * RESIDUAL_RANK]
    layer_w = small_w[:, QUERY_WIDTH + 2 * RESIDUAL_RANK :]
    gains_w = lax.all_gather(norm_gains, "fsdp", axis=1, tiled=True)
    scales = gains_w.astype(F32)
    head_scales = head_gains.astype(F32)

    count = deal_order.shape[0]
    ids = jnp.arange(count, dtype=jnp.int32)
    takes = deal_order[None, :] == ids[:, None]
    slot_of = jnp.sum(jnp.where(takes, ids[None, :], 0), axis=1)
    slot_lens = jnp.sum(jnp.where(takes, lengths[:, None], 0), axis=0)
    earlier = (ids[None, :] < ids[:, None]) & (ids[None, :] // sequences == ids[:, None] // sequences)
    slot_offsets = jnp.sum(jnp.where(earlier, slot_lens[None, :], 0), axis=1)
    offset_of = jnp.sum(jnp.where(takes, slot_offsets[None, :], 0), axis=1)
    group_of = slot_of // sequences
    home_offset = lax.dynamic_slice_in_dim(offset_of, plane * sequences, sequences)
    home_group = lax.dynamic_slice_in_dim(group_of, plane * sequences, sequences)
    home_length = lax.dynamic_slice_in_dim(lengths, plane * sequences, sequences)
    at_position = shard * positions + jnp.arange(positions, dtype=jnp.int32)
    stream = (home_offset[:, None] + at_position[None, :]).reshape(rows_here)
    live = (at_position[None, :] < home_length[:, None]).astype(F32).reshape(rows_here, 1)
    angles = stream.astype(F32)[:, None] * frequencies()[None, :]
    cosine, sine = lax.optimization_barrier((jnp.cos(angles), jnp.sin(angles)))

    far = 1 << 14
    fsdp_sources = over_fsdp.sources(shard)
    fsdp_slots = over_fsdp.slots(shard)
    plane_order = over_rep.sources(plane)
    target = (plane_order[:, None] * sequences + jnp.arange(sequences, dtype=jnp.int32)[None, :]).reshape(-1)
    picks = target[:, None] == ids[None, :]
    target_base = jnp.sum(jnp.where(picks, (group_of * far + offset_of)[None, :], 0), axis=1)
    window_at = shard * window_rows - WINDOW + jnp.arange(window_rows, dtype=jnp.int32)
    target_key = (target_base[:, None] + window_at[None, :]).reshape(-1)
    source_position = fsdp_sources[:, None] * positions + jnp.arange(positions, dtype=jnp.int32)[None, :]
    source_key = jnp.where(
        source_position[:, None, :] < home_length[None, :, None],
        (home_group * far + home_offset)[None, :, None] + source_position[:, None, :],
        -(1 << 20),
    ).reshape(-1)
    window_pick = (target_key[:, None] == source_key[None, :]).astype(BF16)

    blocks = WINDOW // positions + 1
    block_device = shard - (blocks - 1) + jnp.arange(blocks, dtype=jnp.int32)
    device_slot = jnp.sum(
        jnp.where(block_device[:, None] == jnp.arange(shards, dtype=jnp.int32)[None, :], fsdp_slots[None, :], 0),
        axis=1,
    )
    block_slot = jnp.where(block_device >= 0, device_slot, -1)
    pieces = (blocks) * (positions // window_rows)
    piece_index = jnp.clip(
        shard * (positions // window_rows) + jnp.arange(pieces, dtype=jnp.int32), 0, shards - 1
    )
    piece_slot = jnp.sum(
        jnp.where(piece_index[:, None] == jnp.arange(shards, dtype=jnp.int32)[None, :], fsdp_slots[None, :], 0),
        axis=1,
    )
    low = WINDOW - home_offset - shard * positions
    meta = jnp.concatenate([low, block_slot, piece_slot]).astype(jnp.int32)

    x_float = tokens.reshape(rows_here, model_width).astype(F32)
    layer_float = layer_input.reshape(rows_here, PER_LAYER_WIDTH).astype(F32)
    hidden = rms_norm(x_float, scales[0])
    hidden_b = to_low(hidden)
    qkv = dot(hidden_b, in_w)
    query_b, kv_b = heads_fwd(qkv, cosine, sine, head_scales, positions)
    kv_slots = jnp.concatenate(over_fsdp.pieces(kv_b.reshape(sequences, positions, 2 * KEY_WIDTH)), axis=0)
    plane_kv = kv_slots.reshape(shards * rows_here, 2 * KEY_WIDTH)
    window_part = to_low(dot(window_pick, plane_kv)).reshape(planes, sequences, window_rows, 2 * KEY_WIDTH)
    window_here = over_rep.scatter_whole(window_part)[0]
    pw_slots = jnp.concatenate(over_fsdp.pieces(window_here), axis=0)
    kv_slots = kv_slots.reshape(shards, sequences, positions, 2 * KEY_WIDTH)
    pw_slots = pw_slots.reshape(shards, sequences, window_rows, 2 * KEY_WIDTH)
    attended_b = attend_fwd(meta, query_b, kv_slots, pw_slots, dims)
    attn_proj = dot_t(attended_b, out_w)
    laurel_mid_b = to_low(dot(hidden_b, laurel_w[:, :RESIDUAL_RANK]))
    laurel_back = dot_t(laurel_mid_b, laurel_w[:, RESIDUAL_RANK:])
    first_sum = combine(x_float, attn_proj, laurel_back, hidden, scales[1], scales[2])
    ffn_in_b = to_low(rms_norm(first_sum, scales[3]))

    cot_float = cotangent.reshape(rows_here, model_width).astype(F32) * live
    chunks = []
    for i in range(sequences):
        rows = slice(i * positions, (i + 1) * positions)
        with jax.named_scope("gather_in_%d" % i):
            pieces = over_fsdp.pieces(ffn_in_b[rows])
        with jax.named_scope("ffn_fwd_%d" % i):
            (act_b, slope_b, value_b), ffn_in, parts = ffn_fwd(pieces, ffn_w, spans)
        with jax.named_scope("scatter_out_%d" % i):
            down_vals = over_fsdp.scatter(parts).astype(F32)
        second_sum = residual_norm(first_sum[rows], down_vals, scales[4])
        second_b = to_low(second_sum)
        layer_gate = dot(second_b, layer_w[:, :PER_LAYER_WIDTH])
        layer_mix_b = to_low(gated(layer_gate, layer_float[rows]))
        layer_back = dot_t(layer_mix_b, layer_w[:, PER_LAYER_WIDTH:])
        output, pull_out = jax.vjp(residual_norm, second_sum, layer_back, scales[5])
        mixed = to_low(output * live[rows])
        grad_second, grad_layer_back, gain_five = pull_out(cot_float[rows])
        grad_back_b = to_low(grad_layer_back)
        grad_mix = to_low(dot(grad_back_b, layer_w[:, PER_LAYER_WIDTH:])).astype(F32)
        unused_act, pull_act = jax.vjp(gated, layer_gate, layer_float[rows])
        grad_gate_layer, grad_layer_in = pull_act(grad_mix)
        grad_gate_b = to_low(grad_gate_layer)
        grad_second = grad_second + dot_t(grad_gate_b, layer_w[:, :PER_LAYER_WIDTH])
        unused_mid, pull_mid = jax.vjp(residual_norm, first_sum[rows], down_vals, scales[4])
        grad_first, grad_down, gain_four = pull_mid(grad_second)
        with jax.named_scope("gather_grad_%d" % i):
            pieces = over_fsdp.pieces(to_low(grad_down))
        with jax.named_scope("ffn_bwd_%d" % i):
            grad_gate_h, grad_up_h, grad_down_all, parts = ffn_bwd(pieces, ffn_w, slope_b, value_b, spans)
        with jax.named_scope("scatter_grad_%d" % i):
            grad_ffn_in = over_fsdp.scatter(parts).astype(F32)
        unused_pre, pull_pre = jax.vjp(rms_norm, first_sum[rows], scales[3])
        grad_first_b, gain_three = pull_pre(grad_ffn_in)
        chunks.append(
            dict(
                mixed=mixed,
                grad_layer_in=to_low(grad_layer_in),
                grad_first=grad_first + grad_first_b,
                ffn_in=ffn_in,
                act=act_b,
                grad_down=grad_down_all,
                grad_gate=grad_gate_h,
                grad_up=grad_up_h,
                second=second_b,
                grad_gate_layer=grad_gate_b,
                grad_back=grad_back_b,
                layer_mix=layer_mix_b,
                gains=(gain_three, gain_four, gain_five),
            )
        )

    def joined(name):
        return jnp.concatenate([c[name] for c in chunks], axis=0)

    def listed(name):
        return [c[name] for c in chunks]

    row_part = width_here // planes

    def to_owners(parts, kinds, name):
        wide = parts.shape[-1]
        with jax.named_scope("sum_" + name):
            mine = lax.psum_scatter(
                parts.reshape(planes * shards * row_part, wide), "rep", scatter_dimension=0, tiled=True
            )
        with jax.named_scope("deal_" + name):
            theirs = lax.all_to_all(
                mine.reshape(shards, row_part, wide), "fsdp", split_axis=0, concat_axis=0, tiled=True
            )
        theirs = jnp.transpose(theirs.reshape(shards, row_part, kinds, hidden_here), (1, 2, 0, 3))
        with jax.named_scope("spread_" + name):
            whole = lax.all_gather(
                theirs.reshape(row_part, kinds * HIDDEN_UNITS), "rep", axis=0, tiled=True
            )
        return whole.astype(F32)

    with jax.named_scope("down_grad"):
        down_parts = rows_grad(listed("grad_down"), [listed("act")], planes, shards)
    with jax.named_scope("gate_up_grad"):
        gate_up_parts = rows_grad(listed("ffn_in"), [listed("grad_gate"), listed("grad_up")], planes, shards)
    ffn_down_grad = to_owners(down_parts, 1, "down")
    gate_up_grad = to_owners(gate_up_parts, 2, "gate_up")

    grad_first = joined("grad_first")
    unused_comb, pull_combine = jax.vjp(
        combine, x_float, attn_proj, laurel_back, hidden, scales[1], scales[2]
    )
    grad_x_one, grad_proj, grad_laurel, grad_hidden, gain_one, gain_two = pull_combine(grad_first)
    grad_proj_b = to_low(grad_proj)
    grad_laurel_b = to_low(grad_laurel)
    grad_mid_b = to_low(dot(grad_laurel_b, laurel_w[:, RESIDUAL_RANK:]))
    grad_attended_b = to_low(dot(grad_proj_b, out_w))
    with jax.named_scope("small_grad"):
        joined_mid = jnp.concatenate([grad_mid_b, jnp.zeros_like(grad_mid_b)], axis=1)
        mid_joined = jnp.concatenate([jnp.zeros_like(laurel_mid_b), laurel_mid_b], axis=1)
        small_parts = owner_grad(
            fsdp_sources,
            [grad_proj_b, hidden_b, grad_laurel_b, joined("second"), joined("grad_back")],
            [attended_b, joined_mid, mid_joined, joined("grad_gate_layer"), joined("layer_mix")],
            [False, False, True, False, False],
            spans,
        )
    with jax.named_scope("attend_bwd"):
        grad_query, gkv_part, gpw_part = attend_bwd(meta, query_b, kv_slots, pw_slots, grad_attended_b, dims)
    grad_q_b, grad_q_head = heads_bwd(
        qkv, 0, QUERY_HEADS, QUERY_HEADS, cosine, sine, head_scales[0:1], grad_query, positions
    )
    with jax.named_scope("query_grad"):
        query_parts = owner_grad(fsdp_sources, [hidden_b], [grad_q_b], [False], spans)
    with jax.named_scope("window_back"):
        gpw_here = over_fsdp.scatter_whole(gpw_part.reshape(shards * sequences, window_rows, 2 * KEY_WIDTH))
        gpw_all = jnp.concatenate(over_rep.pieces(gpw_here), axis=0).reshape(-1, 2 * KEY_WIDTH)
    gkv_sum = t_dot(window_pick, gpw_all) + gkv_part.reshape(-1, 2 * KEY_WIDTH).astype(F32)
    with jax.named_scope("keys_back"):
        grad_kv = over_fsdp.scatter_whole(
            to_low(gkv_sum).reshape(shards * sequences, positions, 2 * KEY_WIDTH)
        ).reshape(rows_here, 2 * KEY_WIDTH)
    grad_kv_b, grad_k_head = heads_bwd(
        qkv, QUERY_HEADS, 2 * KEY_VALUE_HEADS, KEY_VALUE_HEADS, cosine, sine, head_scales[1:2], grad_kv, positions
    )
    with jax.named_scope("keys_grad"):
        keys_parts = owner_grad(fsdp_sources, [hidden_b], [grad_kv_b], [False], spans)
    grad_hidden = (
        grad_hidden
        + dot_t(grad_mid_b, laurel_w[:, :RESIDUAL_RANK])
        + dot_t(grad_q_b, in_w[:, :QUERY_WIDTH])
        + dot_t(grad_kv_b, in_w[:, QUERY_WIDTH:])
    )
    unused_norm, pull_in = jax.vjp(rms_norm, x_float, scales[0])
    grad_x_two, gain_zero = pull_in(grad_hidden)
    input_grad = to_low(grad_x_one + grad_x_two).reshape(tokens.shape)

    def owned(parts, name):
        with jax.named_scope("own_" + name):
            mine = over_fsdp.scatter(parts)[0]
        with jax.named_scope("all_" + name):
            return lax.psum(mine, "rep").astype(F32)

    small_grad = owned(small_parts, "small")
    query_grad = owned(query_parts, "query")
    keys_grad = owned(keys_parts, "keys")
    attn_in_grad = jnp.concatenate([query_grad, keys_grad], axis=1)

    gain_rows = jnp.stack(
        [gain_zero, gain_one, gain_two] + [sum(c["gains"][k] for c in chunks) for k in range(3)]
    )
    grad_head = jnp.concatenate([grad_q_head, grad_k_head], axis=0)
    packed = jnp.concatenate([gain_rows, jnp.pad(grad_head, ((0, 0), (0, model_width - HEAD_DIM)))], axis=0)
    packed = over_rep.total(over_fsdp.total(packed))
    gain_share = lax.dynamic_slice_in_dim(packed[:6], shard * width_here, width_here, 1)
    return (
        jnp.stack([c["mixed"] for c in chunks]),
        input_grad,
        jnp.stack([c["grad_layer_in"] for c in chunks]),
        attn_in_grad,
        small_grad[:, :QUERY_WIDTH],
        gate_up_grad,
        ffn_down_grad,
        small_grad[:, QUERY_WIDTH : QUERY_WIDTH + 2 * RESIDUAL_RANK],
        small_grad[:, QUERY_WIDTH + 2 * RESIDUAL_RANK :],
        gain_share,
        packed[6:8, :HEAD_DIM],
    )


def solution(mesh):
    rows = P("rep", "fsdp", None)
    weight = P("fsdp", None)
    return jax.shard_map(
        on_device,
        mesh=mesh,
        in_specs=(rows, rows, rows, P(), P()) + (weight,) * 6 + (P(None, "fsdp"), P()),
        out_specs=(rows, rows, rows) + (weight,) * 6 + (P(None, "fsdp"), P()),
        check_vma=False,
    )
```

```python
import jax
import jax.numpy as jnp
import numpy as np
from jax import lax
from jax.experimental import pallas as pl
from jax.experimental.pallas import tpu as pltpu
from jax.sharding import PartitionSpec as P

QUERY_HEADS = 8
KEY_VALUE_HEADS = 2
HEADS_PER_KEY = QUERY_HEADS // KEY_VALUE_HEADS
HEAD_DIM = 256
HALF_DIM = HEAD_DIM // 2
HIDDEN_UNITS = 8192
RESIDUAL_RANK = 64
PER_LAYER_WIDTH = 256
WINDOW = 512
QUERY_WIDTH = QUERY_HEADS * HEAD_DIM
KEY_WIDTH = KEY_VALUE_HEADS * HEAD_DIM

EPS = 1e-06
BASE = 10000.0
ROOT_HALF = 0.7071067811865476
NEG_FILL = -1e30
SCALE = HEAD_DIM ** (-0.5)

F32 = jnp.float32
BF16 = jnp.bfloat16


def rms_norm(values, scales):
    return values * lax.rsqrt(jnp.mean(values * values, axis=-1, keepdims=True) + EPS) * scales


def gelu_tanh(values):
    return jax.nn.gelu(values, approximate=True)


def frequencies():
    return 1.0 / BASE ** (jnp.arange(HALF_DIM, dtype=F32) * 2.0 / HEAD_DIM)


def combine(x_float, attn_proj, laurel_back, hidden, scale_one, scale_two):
    return (
        x_float + rms_norm(attn_proj, scale_two) + hidden + rms_norm(laurel_back, scale_one)
    ) * ROOT_HALF


def gated(gate, up):
    return gelu_tanh(gate) * up


def residual_norm(base, values, scales):
    return base + rms_norm(values, scales)


def to_low(values):
    return values.astype(BF16)


def dot(left, right):
    return jnp.dot(left, right, preferred_element_type=F32)


def dot_t(left, right):
    return lax.dot_general(left, right, (((1,), (1,)), ((), ())), preferred_element_type=F32)


def t_dot(left, right):
    return lax.dot_general(left, right, (((0,), (0,)), ((), ())), preferred_element_type=F32)


def fsdp_phases(count):
    bits = [1 << k for k in range(1, count.bit_length() - 1)]
    phases = []
    for k in range(len(bits)):
        phases.append([i ^ (bits[k] if i % 2 == 0 else bits[len(bits) - 1 - k]) for i in range(count)])
    phases.append([i ^ 1 for i in range(count)])
    return phases


def rep_phases(count):
    bits = [1 << k for k in range(count.bit_length() - 1)]
    return [[i ^ b for i in range(count)] for b in reversed(bits)]


def slot_table(phases, count):
    held = [[i] for i in range(count)]
    for perm in phases:
        held = [held[i] + held[perm[i]] for i in range(count)]
    return np.array(held, dtype=np.int32).T


class Exchange:
    def __init__(self, axis, phases, count):
        self.axis = axis
        self.count = count
        self.perms = [[(i, p[i]) for i in range(count)] for p in phases]
        self.table = slot_table(phases, count)
        inverse = np.zeros_like(self.table)
        for i in range(count):
            inverse[self.table[:, i], i] = np.arange(count)
        self.inverse = inverse

    def sources(self, index):
        return lax.dynamic_index_in_dim(jnp.asarray(self.table), index, 1, keepdims=False)

    def slots(self, index):
        return lax.dynamic_index_in_dim(jnp.asarray(self.inverse), index, 1, keepdims=False)

    def pieces(self, piece):
        held = [piece]
        for perm in self.perms:
            held = held + [lax.ppermute(h, self.axis, perm) for h in held]
        return held

    def groups(self):
        return [(0, 1)] + [(1 << k, 2 << k) for k in range(len(self.perms))]

    def scatter(self, parts):
        mine, got = self.scatter_pair(parts)
        return (mine.astype(F32) + got.astype(F32)).astype(mine.dtype)

    def scatter_pair(self, parts):
        spans = self.groups()
        for k in range(len(self.perms), 0, -1):
            got = lax.ppermute(parts[k], self.axis, self.perms[k - 1])
            if k == 1:
                return parts[0], got
            step = got.shape[0] // spans[k][0]
            parts = [
                (parts[j].astype(F32) + got[spans[j][0] * step : spans[j][1] * step].astype(F32)).astype(got.dtype)
                for j in range(k)
            ]

    def scatter_whole(self, whole):
        step = whole.shape[0] // self.count
        return self.scatter([whole[lo * step : hi * step] for lo, hi in self.groups()])

    def total(self, value):
        for perm in self.perms:
            value = value + lax.ppermute(value, self.axis, perm)
        return value


def line_gather(piece, axis, count):
    right, left = [piece], [piece]
    for s in range(1, count):
        right.append(lax.ppermute(right[-1], axis, [(i, i + 1) for i in range(s - 1, count - 1)]))
        left.append(lax.ppermute(left[-1], axis, [(i, i - 1) for i in range(1, count - s + 1)]))
    return [piece] + [right[count - r] + left[r] for r in range(1, count)]


def after(value, *others):
    return lax.optimization_barrier((value, *others))[0]


def heads_fwd_body(qkv_ref, cos_ref, sin_ref, gains_ref, q_ref, kv_ref):
    cosine = cos_ref[...]
    sine = sin_ref[...]
    for c in range(QUERY_HEADS + 2 * KEY_VALUE_HEADS):
        head = qkv_ref[:, c * HEAD_DIM : (c + 1) * HEAD_DIM]
        normed = head * lax.rsqrt(jnp.mean(head * head, axis=-1, keepdims=True) + EPS)
        if c < QUERY_HEADS + KEY_VALUE_HEADS:
            row = 0 if c < QUERY_HEADS else 1
            normed = normed * gains_ref[row : row + 1, :]
            low = normed[:, :HALF_DIM]
            high = normed[:, HALF_DIM:]
            first = to_low(low * cosine - high * sine)
            second = to_low(high * cosine + low * sine)
        else:
            first = to_low(normed[:, :HALF_DIM])
            second = to_low(normed[:, HALF_DIM:])
        if c < QUERY_HEADS:
            q_ref[:, c * HEAD_DIM : c * HEAD_DIM + HALF_DIM] = first
            q_ref[:, c * HEAD_DIM + HALF_DIM : (c + 1) * HEAD_DIM] = second
        else:
            at = (c - QUERY_HEADS) * HEAD_DIM
            kv_ref[:, at : at + HALF_DIM] = first
            kv_ref[:, at + HALF_DIM : at + HEAD_DIM] = second


def heads_fwd(qkv, cosine, sine, head_scales, block):
    rows, width = qkv.shape
    return pl.pallas_call(
        heads_fwd_body,
        grid=(rows // block,),
        in_specs=[
            pl.BlockSpec((block, width), lambda i: (i, 0)),
            pl.BlockSpec((block, HALF_DIM), lambda i: (i, 0)),
            pl.BlockSpec((block, HALF_DIM), lambda i: (i, 0)),
            pl.BlockSpec((2, HEAD_DIM), lambda i: (0, 0)),
        ],
        out_specs=[
            pl.BlockSpec((block, QUERY_WIDTH), lambda i: (i, 0)),
            pl.BlockSpec((block, 2 * KEY_WIDTH), lambda i: (i, 0)),
        ],
        out_shape=[
            jax.ShapeDtypeStruct((rows, QUERY_WIDTH), BF16),
            jax.ShapeDtypeStruct((rows, 2 * KEY_WIDTH), BF16),
        ],
        name="heads_fwd",
    )(qkv, cosine, sine, head_scales)


def heads_bwd_body(heads, gained, qkv_ref, cos_ref, sin_ref, gains_ref, grad_ref, out_ref, gain_ref):
    @pl.when(pl.program_id(0) == 0)
    def _():
        gain_ref[...] = jnp.zeros_like(gain_ref)

    cosine = cos_ref[...]
    sine = sin_ref[...]
    total = jnp.zeros((1, HEAD_DIM), F32)
    for c in range(heads):
        here = slice(c * HEAD_DIM, (c + 1) * HEAD_DIM)
        head = qkv_ref[:, here]
        scale = lax.rsqrt(jnp.mean(head * head, axis=-1, keepdims=True) + EPS)
        normed = head * scale
        grad = grad_ref[:, here].astype(F32)
        if c < gained:
            first = grad[:, :HALF_DIM]
            second = grad[:, HALF_DIM:]
            grad = jnp.concatenate(
                [first * cosine + second * sine, second * cosine - first * sine], axis=1
            )
            total = total + jnp.sum(grad * normed, axis=0, keepdims=True)
            grad = grad * gains_ref[...]
        back = scale * (grad - normed * jnp.mean(grad * normed, axis=-1, keepdims=True))
        out_ref[:, here] = to_low(back)
    gain_ref[...] += total


def heads_bwd(qkv, first, heads, gained, cosine, sine, head_scale, grad, block):
    rows = qkv.shape[0]
    width = heads * HEAD_DIM
    at = first // heads
    return pl.pallas_call(
        lambda *refs: heads_bwd_body(heads, gained, *refs),
        grid=(rows // block,),
        in_specs=[
            pl.BlockSpec((block, width), lambda i: (i, at)),
            pl.BlockSpec((block, HALF_DIM), lambda i: (i, 0)),
            pl.BlockSpec((block, HALF_DIM), lambda i: (i, 0)),
            pl.BlockSpec((1, HEAD_DIM), lambda i: (0, 0)),
            pl.BlockSpec((block, width), lambda i: (i, 0)),
        ],
        out_specs=[
            pl.BlockSpec((block, width), lambda i: (i, 0)),
            pl.BlockSpec((1, HEAD_DIM), lambda i: (0, 0)),
        ],
        out_shape=[
            jax.ShapeDtypeStruct((rows, width), BF16),
            jax.ShapeDtypeStruct((1, HEAD_DIM), F32),
        ],
        name="heads_bwd",
    )(qkv, cosine, sine, head_scale, grad)


def load_window(meta_ref, kv_ref, pw_ref, keys_ref, sequences, positions, window_rows, shards):
    blocks = WINDOW // positions + 1
    per_block = positions // window_rows
    for b in range(blocks):
        slot = meta_ref[sequences + b]

        @pl.when(slot >= 0)
        def _():
            keys_ref[b * positions : (b + 1) * positions, :] = kv_ref[jnp.maximum(slot, 0), 0]

        @pl.when(slot < 0)
        def _():
            for m in range(per_block):
                piece = meta_ref[sequences + blocks + b * per_block + m]
                at = b * positions + m * window_rows
                keys_ref[at : at + window_rows, :] = pw_ref[piece, 0]


def window_mask(meta_ref, positions):
    width = WINDOW + positions
    row = lax.broadcasted_iota(jnp.int32, (positions, width), 0)
    col = lax.broadcasted_iota(jnp.int32, (positions, width), 1)
    low = meta_ref[pl.program_id(0)]
    return (col > row) & (col <= row + WINDOW) & (col >= low)


def head_probs(query, keys, allowed):
    scores = dot_t(query, keys) * SCALE
    masked = jnp.where(allowed, scores, NEG_FILL)
    top = jnp.max(masked, axis=-1, keepdims=True)
    powers = jnp.exp(masked - top)
    return powers / jnp.sum(powers, axis=-1, keepdims=True)


def attend_fwd_body(sequences, positions, window_rows, shards, meta_ref, q_ref, kv_ref, pw_ref, o_ref, keys_ref):
    load_window(meta_ref, kv_ref, pw_ref, keys_ref, sequences, positions, window_rows, shards)
    allowed = window_mask(meta_ref, positions)
    for a in range(KEY_VALUE_HEADS):
        keys = keys_ref[:, a * HEAD_DIM : (a + 1) * HEAD_DIM]
        vals = keys_ref[:, KEY_WIDTH + a * HEAD_DIM : KEY_WIDTH + (a + 1) * HEAD_DIM]
        for g in range(HEADS_PER_KEY):
            c = a * HEADS_PER_KEY + g
            probs = head_probs(q_ref[:, c * HEAD_DIM : (c + 1) * HEAD_DIM], keys, allowed)
            o_ref[:, c * HEAD_DIM : (c + 1) * HEAD_DIM] = to_low(dot(to_low(probs), vals))


def attend_bwd_body(
    sequences, positions, window_rows, shards,
    meta_ref, q_ref, kv_ref, pw_ref, go_ref, gq_ref, gkv_ref, gpw_ref, keys_ref, grads_ref,
):
    load_window(meta_ref, kv_ref, pw_ref, keys_ref, sequences, positions, window_rows, shards)
    allowed = window_mask(meta_ref, positions)
    for a in range(KEY_VALUE_HEADS):
        keys = keys_ref[:, a * HEAD_DIM : (a + 1) * HEAD_DIM]
        vals = keys_ref[:, KEY_WIDTH + a * HEAD_DIM : KEY_WIDTH + (a + 1) * HEAD_DIM]
        grad_keys = jnp.zeros((WINDOW + positions, HEAD_DIM), F32)
        grad_vals = jnp.zeros((WINDOW + positions, HEAD_DIM), F32)
        for g in range(HEADS_PER_KEY):
            c = a * HEADS_PER_KEY + g
            query = q_ref[:, c * HEAD_DIM : (c + 1) * HEAD_DIM]
            grad_out = go_ref[:, c * HEAD_DIM : (c + 1) * HEAD_DIM]
            probs = head_probs(query, keys, allowed)
            grad_probs = dot_t(grad_out, vals)
            delta = jnp.sum(probs * grad_probs, axis=-1, keepdims=True)
            grad_scores = to_low(probs * (grad_probs - delta))
            gq_ref[:, c * HEAD_DIM : (c + 1) * HEAD_DIM] = dot(grad_scores, keys) * SCALE
            grad_keys = grad_keys + t_dot(grad_scores, query)
            grad_vals = grad_vals + t_dot(to_low(probs), grad_out)
        grads_ref[:, a * HEAD_DIM : (a + 1) * HEAD_DIM] = to_low(grad_keys * SCALE)
        grads_ref[:, KEY_WIDTH + a * HEAD_DIM : KEY_WIDTH + (a + 1) * HEAD_DIM] = to_low(grad_vals)
    gkv_ref[...] = jnp.zeros_like(gkv_ref)
    gpw_ref[...] = jnp.zeros_like(gpw_ref)
    blocks = WINDOW // positions + 1
    per_block = positions // window_rows
    for b in range(blocks):
        slot = meta_ref[sequences + b]

        @pl.when(slot >= 0)
        def _():
            gkv_ref[jnp.maximum(slot, 0), 0] = grads_ref[b * positions : (b + 1) * positions, :]

        @pl.when(slot < 0)
        def _():
            for m in range(per_block):
                piece = meta_ref[sequences + blocks + b * per_block + m]
                at = b * positions + m * window_rows
                gpw_ref[piece, 0] = grads_ref[at : at + window_rows, :]


def attention_specs(sequences, positions, window_rows, shards):
    rows = pl.BlockSpec((positions, QUERY_WIDTH), lambda i, m: (i, 0))
    kv = pl.BlockSpec((shards, 1, positions, 2 * KEY_WIDTH), lambda i, m: (0, i, 0, 0))
    pw = pl.BlockSpec((shards, 1, window_rows, 2 * KEY_WIDTH), lambda i, m: (0, i, 0, 0))
    return rows, kv, pw


def attend_fwd(meta, query, kv_slots, pw_slots, dims):
    sequences, positions, window_rows, shards = dims
    rows, kv, pw = attention_specs(*dims)
    return pl.pallas_call(
        lambda *refs: attend_fwd_body(*dims, *refs),
        grid_spec=pltpu.PrefetchScalarGridSpec(
            num_scalar_prefetch=1,
            grid=(sequences,),
            in_specs=[rows, kv, pw],
            out_specs=rows,
            scratch_shapes=[pltpu.VMEM((WINDOW + positions, 2 * KEY_WIDTH), BF16)],
        ),
        out_shape=jax.ShapeDtypeStruct((sequences * positions, QUERY_WIDTH), BF16),
        name="attend_fwd",
    )(meta, query, kv_slots, pw_slots)


def attend_bwd(meta, query, kv_slots, pw_slots, grad_out, dims):
    sequences, positions, window_rows, shards = dims
    rows, kv, pw = attention_specs(*dims)
    return pl.pallas_call(
        lambda *refs: attend_bwd_body(*dims, *refs),
        grid_spec=pltpu.PrefetchScalarGridSpec(
            num_scalar_prefetch=1,
            grid=(sequences,),
            in_specs=[rows, kv, pw, rows],
            out_specs=[rows, kv, pw],
            scratch_shapes=[
                pltpu.VMEM((WINDOW + positions, 2 * KEY_WIDTH), BF16),
                pltpu.VMEM((WINDOW + positions, 2 * KEY_WIDTH), BF16),
            ],
        ),
        out_shape=[
            jax.ShapeDtypeStruct((sequences * positions, QUERY_WIDTH), F32),
            jax.ShapeDtypeStruct(kv_slots.shape, BF16),
            jax.ShapeDtypeStruct(pw_slots.shape, BF16),
        ],
        name="attend_bwd",
    )(meta, query, kv_slots, pw_slots, grad_out)


GELU_A = 0.7978845608028654
GELU_B = 0.044715


def take_slots(refs, all_ref, step, rows):
    each = all_ref.shape[0] // rows
    for k, ref in enumerate(refs):

        @pl.when(step == k // each)
        def _():
            at = (k % each) * rows
            all_ref[at : at + rows, :] = ref[...]


def give_slots(result, spans, out_refs, step, rows):
    each = result.shape[0] // rows
    for (lo, hi), ref in zip(spans, out_refs):
        for k in range(lo, hi):

            @pl.when(step == k // each)
            def _():
                at = (k % each) * rows
                ref[(k - lo) * rows : (k - lo + 1) * rows, :] = result[at : at + rows, :]


def ffn_fwd_body(shards, spans, *refs):
    x_refs = refs[:shards]
    w_ref = refs[shards]
    act_ref, slope_ref, value_ref, all_ref = refs[shards + 1 : shards + 5]
    out_refs = refs[shards + 5 :]
    rows = x_refs[0].shape[0]
    hidden = w_ref.shape[1] // 3
    step = pl.program_id(0)
    take_slots(x_refs, all_ref, step, rows)
    inputs = all_ref[...]
    gate = dot(inputs, w_ref[:, :hidden])
    up = dot(inputs, w_ref[:, hidden : 2 * hidden])
    squared = gate * gate
    bend = jnp.tanh(GELU_A * gate * (1.0 + GELU_B * squared))
    half = 0.5 * (1.0 + bend)
    value = gate * half
    slope = half + (0.5 * GELU_A) * gate * (1.0 - bend * bend) * (1.0 + 3.0 * GELU_B * squared)
    act = to_low(value * up)
    act_ref[...] = act
    slope_ref[...] = to_low(slope * up)
    value_ref[...] = to_low(value)
    give_slots(to_low(dot_t(act, w_ref[:, 2 * hidden :])), spans, out_refs, step, rows)


def ffn_specs(shards, rows, width, hidden, spans):
    every = shards * rows
    block = min(256, every)
    row = lambda n: pl.BlockSpec((block, n), lambda j: (j, 0))
    pieces = [pl.BlockSpec((rows, width), lambda j: (0, 0))] * shards
    weights = pl.BlockSpec((width, 3 * hidden), lambda j: (0, 0), pipeline_mode=pl.Buffered(1))
    groups = [pl.BlockSpec(((hi - lo) * rows, width), lambda j: (0, 0)) for lo, hi in spans]
    shapes = [jax.ShapeDtypeStruct(((hi - lo) * rows, width), BF16) for lo, hi in spans]
    return every, every // block, row, pieces, weights, groups, shapes


def ffn_fwd(pieces, weights, spans):
    shards = len(pieces)
    rows, width = pieces[0].shape
    hidden = weights.shape[1] // 3
    every, steps, row, piece_specs, weight_spec, groups, group_shapes = ffn_specs(shards, rows, width, hidden, spans)
    outs = pl.pallas_call(
        lambda *refs: ffn_fwd_body(shards, spans, *refs),
        grid=(steps,),
        in_specs=piece_specs + [weight_spec],
        out_specs=[row(hidden)] * 3 + [row(width)] + groups,
        out_shape=[jax.ShapeDtypeStruct((every, hidden), BF16)] * 3
        + [jax.ShapeDtypeStruct((every, width), BF16)]
        + group_shapes,
        compiler_params=pltpu.CompilerParams(vmem_limit_bytes=60 << 20),
        cost_estimate=pl.CostEstimate(
            flops=6 * every * width * hidden, transcendentals=every * hidden,
            bytes_accessed=2 * (3 * width * hidden + 3 * every * width + 3 * every * hidden),
        ),
        name="ffn_fwd",
    )(*pieces, weights)
    return outs[:3], outs[3], outs[4:]


def ffn_bwd_body(shards, spans, *refs):
    g_refs = refs[:shards]
    w_ref, slope_ref, value_ref = refs[shards : shards + 3]
    gg_ref, gu_ref = refs[shards + 3 : shards + 5]
    out_refs = refs[shards + 5 : -1]
    all_ref = refs[-1]
    rows = g_refs[0].shape[0]
    hidden = w_ref.shape[1] // 3
    step = pl.program_id(0)
    take_slots(g_refs, all_ref, step, rows)
    grad = to_low(dot(all_ref[...], w_ref[:, 2 * hidden :])).astype(F32)
    grad_gate = to_low(grad * slope_ref[...].astype(F32))
    grad_up = to_low(grad * value_ref[...].astype(F32))
    gg_ref[...] = grad_gate
    gu_ref[...] = grad_up
    back = dot_t(grad_gate, w_ref[:, :hidden]) + dot_t(grad_up, w_ref[:, hidden : 2 * hidden])
    give_slots(to_low(back), spans, out_refs, step, rows)


def ffn_bwd(pieces, weights, slope, value, spans):
    shards = len(pieces)
    rows, width = pieces[0].shape
    hidden = weights.shape[1] // 3
    every, steps, row, piece_specs, weight_spec, groups, group_shapes = ffn_specs(shards, rows, width, hidden, spans)
    outs = pl.pallas_call(
        lambda *refs: ffn_bwd_body(shards, spans, *refs),
        grid=(steps,),
        in_specs=piece_specs + [weight_spec] + [row(hidden)] * 2,
        out_specs=[row(hidden)] * 2 + groups,
        out_shape=[jax.ShapeDtypeStruct((every, hidden), BF16)] * 2 + group_shapes,
        scratch_shapes=[pltpu.VMEM((every // steps, width), BF16)],
        compiler_params=pltpu.CompilerParams(vmem_limit_bytes=60 << 20),
        cost_estimate=pl.CostEstimate(
            flops=6 * every * width * hidden, transcendentals=0,
            bytes_accessed=2 * (3 * width * hidden + 3 * every * width + 4 * every * hidden),
        ),
        name="ffn_bwd",
    )(*pieces, weights, slope, value)
    return outs[0], outs[1], outs[2:]


def inverse_rms(values):
    return lax.rsqrt(jnp.mean(values * values, axis=-1, keepdims=True) + EPS)


def norm_back(inverse, unit, grad):
    return inverse * (grad - unit * jnp.mean(grad * unit, axis=-1, keepdims=True))


def middle_body(mine_ref, got_ref, first_ref, cot_ref, live_ref, layer_ref, w_ref, gains_ref, *outs):
    mixed_ref, glayer_ref, second_ref, ggate_ref, gback_ref, mix_ref, gdown_ref, gfirst_ref, gain_ref = outs
    live = live_ref[...]
    down = mine_ref[...].astype(F32) + got_ref[...].astype(F32)
    down_inv = inverse_rms(down)
    down_unit = down * down_inv
    second = first_ref[...] + down_unit * gains_ref[4:5, :]
    second_b = to_low(second)
    second_ref[...] = second_b
    layer = layer_ref[...].astype(F32)
    gate = dot(second_b, w_ref[:, :PER_LAYER_WIDTH])
    squared = gate * gate
    bend = jnp.tanh(GELU_A * gate * (1.0 + GELU_B * squared))
    half = 0.5 * (1.0 + bend)
    value = gate * half
    slope = half + (0.5 * GELU_A) * gate * (1.0 - bend * bend) * (1.0 + 3.0 * GELU_B * squared)
    mix = to_low(value * layer)
    mix_ref[...] = mix
    back = dot_t(mix, w_ref[:, PER_LAYER_WIDTH:])
    back_inv = inverse_rms(back)
    back_unit = back * back_inv
    mixed_ref[...] = to_low((second + back_unit * gains_ref[5:6, :]) * live)
    grad = cot_ref[...].astype(F32) * live
    gain_ref[1:2, :] = jnp.sum(grad * back_unit, axis=0, keepdims=True)
    grad_back = to_low(norm_back(back_inv, back_unit, grad * gains_ref[5:6, :]))
    gback_ref[...] = grad_back
    grad_mix = to_low(dot(grad_back, w_ref[:, PER_LAYER_WIDTH:])).astype(F32)
    glayer_ref[...] = to_low(grad_mix * value)
    grad_gate = to_low(grad_mix * layer * slope)
    ggate_ref[...] = grad_gate
    grad = grad + dot_t(grad_gate, w_ref[:, :PER_LAYER_WIDTH])
    gfirst_ref[...] = grad
    gain_ref[0:1, :] = jnp.sum(grad * down_unit, axis=0, keepdims=True)
    gdown_ref[...] = to_low(norm_back(down_inv, down_unit, grad * gains_ref[4:5, :]))


def middle(index, rows, mine, got, first_sum, cot, live, layer, weights, gains):
    width = first_sum.shape[1]
    at = lambda n: pl.BlockSpec((rows, n), lambda z: (index, 0))
    own = lambda r, n: pl.BlockSpec((r, n), lambda z: (0, 0))
    low = lambda n: jax.ShapeDtypeStruct((rows, n), BF16)
    return pl.pallas_call(
        middle_body,
        grid=(1,),
        in_specs=[own(rows, width), own(rows, width), at(width), at(width), at(1), at(PER_LAYER_WIDTH)]
        + [own(width, 2 * PER_LAYER_WIDTH), own(6, width)],
        out_specs=[own(rows, width), own(rows, PER_LAYER_WIDTH), own(rows, width), own(rows, PER_LAYER_WIDTH)]
        + [own(rows, width), own(rows, PER_LAYER_WIDTH), own(rows, width), own(rows, width), own(2, width)],
        out_shape=[low(width), low(PER_LAYER_WIDTH), low(width), low(PER_LAYER_WIDTH)]
        + [low(width), low(PER_LAYER_WIDTH), low(width)]
        + [jax.ShapeDtypeStruct((rows, width), F32), jax.ShapeDtypeStruct((2, width), F32)],
        compiler_params=pltpu.CompilerParams(vmem_limit_bytes=60 << 20),
        cost_estimate=pl.CostEstimate(
            flops=8 * rows * width * PER_LAYER_WIDTH, transcendentals=rows * PER_LAYER_WIDTH,
            bytes_accessed=rows * width * 22 + width * PER_LAYER_WIDTH * 4,
        ),
        name="middle",
    )(mine, got, first_sum, cot, live, layer, weights, gains)


def first_back_body(chunks, *refs):
    mine_refs = refs[:chunks]
    got_refs = refs[chunks : 2 * chunks]
    gfirst_refs = refs[2 * chunks : 3 * chunks]
    first_ref, att_ref, lo_ref, gains_ref = refs[3 * chunks : 3 * chunks + 4]
    gsum_ref, gatt_ref, glo_ref, gain_ref, grad_ref, base_ref = refs[3 * chunks + 4 :]
    step = pl.program_id(0)
    for c in range(chunks):

        @pl.when(step == c)
        def _():
            grad_ref[...] = mine_refs[c][...].astype(F32) + got_refs[c][...].astype(F32)
            base_ref[...] = gfirst_refs[c][...]

    first = first_ref[...]
    inverse = inverse_rms(first)
    unit = first * inverse
    grad = grad_ref[...]
    gain_three = jnp.sum(grad * unit, axis=0, keepdims=True)
    grad = (base_ref[...] + norm_back(inverse, unit, grad * gains_ref[3:4, :])) * ROOT_HALF
    gsum_ref[...] = grad
    att = att_ref[...]
    inverse = inverse_rms(att)
    unit = att * inverse
    gain_two = jnp.sum(grad * unit, axis=0, keepdims=True)
    gatt_ref[...] = to_low(norm_back(inverse, unit, grad * gains_ref[2:3, :]))
    low = lo_ref[...]
    inverse = inverse_rms(low)
    unit = low * inverse
    gain_one = jnp.sum(grad * unit, axis=0, keepdims=True)
    glo_ref[...] = to_low(norm_back(inverse, unit, grad * gains_ref[1:2, :]))
    gains = jnp.concatenate([gain_one, gain_two, gain_three], axis=0)

    @pl.when(step == 0)
    def _():
        gain_ref[...] = gains

    @pl.when(step > 0)
    def _():
        gain_ref[...] += gains


def first_back(mines, gots, gfirsts, first_sum, att, low, gains):
    chunks = len(mines)
    rows, width = mines[0].shape
    whole = pl.BlockSpec((rows, width), lambda c: (0, 0))
    row = pl.BlockSpec((rows, width), lambda c: (c, 0))
    every = chunks * rows
    return pl.pallas_call(
        lambda *refs: first_back_body(chunks, *refs),
        grid=(chunks,),
        in_specs=[whole] * (3 * chunks) + [row] * 3 + [pl.BlockSpec((6, width), lambda c: (0, 0))],
        out_specs=[row] * 3 + [pl.BlockSpec((3, width), lambda c: (0, 0))],
        out_shape=[
            jax.ShapeDtypeStruct((every, width), F32),
            jax.ShapeDtypeStruct((every, width), BF16),
            jax.ShapeDtypeStruct((every, width), BF16),
            jax.ShapeDtypeStruct((3, width), F32),
        ],
        scratch_shapes=[pltpu.VMEM((rows, width), F32)] * 2,
        compiler_params=pltpu.CompilerParams(vmem_limit_bytes=60 << 20),
        cost_estimate=pl.CostEstimate(
            flops=30 * every * width, transcendentals=0, bytes_accessed=every * width * 28
        ),
        name="first_back",
    )(*mines, *gots, *gfirsts, first_sum, att, low, gains)


def join_rows_body(parity_ref, both_ref, mine_ref, other_ref, out_ref):
    half = both_ref.shape[1]
    quarter = half // 2
    out_ref[0, :half, :] = both_ref[0]

    @pl.when(parity_ref[0] == 0)
    def _():
        out_ref[0, half : half + quarter, :] = mine_ref[0]
        out_ref[0, half + quarter :, :] = other_ref[0]

    @pl.when(parity_ref[0] != 0)
    def _():
        out_ref[0, half : half + quarter, :] = other_ref[0]
        out_ref[0, half + quarter :, :] = mine_ref[0]


def join_rows(parity, both, mine, other):
    shards, half, wide = both.shape
    block = lambda n: pl.BlockSpec((1, n, wide), lambda f, p: (f, 0, 0))
    return pl.pallas_call(
        join_rows_body,
        grid_spec=pltpu.PrefetchScalarGridSpec(
            num_scalar_prefetch=1,
            grid=(shards,),
            in_specs=[block(half), block(half // 2), block(half // 2)],
            out_specs=block(2 * half),
        ),
        out_shape=jax.ShapeDtypeStruct((shards, 2 * half, wide), BF16),
        cost_estimate=pl.CostEstimate(flops=0, transcendentals=0, bytes_accessed=8 * shards * half * wide),
        name="join_rows",
    )(parity, both, mine, other)


def rows_grad_body(planes, chunks, count, kinds, *refs):
    lefts = refs[: chunks * count]
    rights = refs[chunks * count : chunks * (count + kinds)]
    out, left_ref = refs[-2:]
    size = lefts[0].shape[0]
    for n, ref in enumerate(lefts):
        left_ref[n * size : (n + 1) * size, :] = ref[...]
    every = size * count
    for k in range(kinds):
        total = t_dot(left_ref[:every, :], rights[k * chunks][...])
        for c in range(1, chunks):
            total = total + t_dot(left_ref[c * every : (c + 1) * every, :], rights[k * chunks + c][...])
        total = to_low(total)
        rows, hidden = total.shape[0] // planes, total.shape[1]
        for q in range(planes):
            out[q, 0, :, k * hidden : (k + 1) * hidden] = total[q * rows : (q + 1) * rows, :]


def rows_grad(lefts, kinds, planes, shards):
    chunks = len(lefts)
    count = len(lefts[0])
    rows, width = lefts[0][0].shape
    block = width // shards
    flat = [r for rights in kinds for r in rights]
    every, hidden = flat[0].shape
    part = block // planes
    wide = len(kinds) * hidden
    return pl.pallas_call(
        lambda *refs: rows_grad_body(planes, chunks, count, len(kinds), *refs),
        grid=(shards,),
        in_specs=[pl.BlockSpec((rows, block), lambda f: (0, f))] * (chunks * count)
        + [pl.BlockSpec((every, hidden), lambda f: (0, 0), pipeline_mode=pl.Buffered(1))] * len(flat),
        out_specs=pl.BlockSpec((planes, 1, part, wide), lambda f: (0, f, 0, 0)),
        out_shape=jax.ShapeDtypeStruct((planes, shards, part, wide), BF16),
        scratch_shapes=[pltpu.VMEM((chunks * every, block), BF16)],
        compiler_params=pltpu.CompilerParams(vmem_limit_bytes=60 << 20),
        cost_estimate=pl.CostEstimate(
            flops=2 * chunks * every * width * wide, transcendentals=0,
            bytes_accessed=2 * (chunks * every * (width + wide) + width * wide),
        ),
        name="rows_grad",
    )(*[p for pieces in lefts for p in pieces], *flat)


def owner_grad_body(pairs, spans, order_ref, *refs):
    lefts = refs[: len(pairs)]
    rights = refs[len(pairs) : 2 * len(pairs)]
    outs = refs[2 * len(pairs) :]
    step = pl.program_id(0)
    for ref, (lo, hi) in zip(outs, spans):

        @pl.when((step >= lo) & (step < hi))
        def _():
            at = 0
            parts = []
            for n, (left, right) in enumerate(zip(lefts, rights)):
                value = t_dot(left[...], right[...])
                if pairs[n]:
                    parts[-1] = parts[-1] + value
                else:
                    parts.append(value)
            for value in parts:
                ref[0, :, at : at + value.shape[1]] = to_low(value)
                at += value.shape[1]


def owner_grad(order, lefts, rights, joins, spans):
    shards = spans[-1][1]
    rows, width = lefts[0].shape
    block = width // shards
    total = sum(r.shape[1] for r, j in zip(rights, joins) if not j)
    return pl.pallas_call(
        lambda *refs: owner_grad_body(joins, spans, *refs),
        grid_spec=pltpu.PrefetchScalarGridSpec(
            num_scalar_prefetch=1,
            grid=(shards,),
            in_specs=[pl.BlockSpec((rows, block), lambda t, o: (0, o[t]))] * len(lefts)
            + [pl.BlockSpec(r.shape, lambda t, o: (0, 0)) for r in rights],
            out_specs=[
                pl.BlockSpec((1, block, total), lambda t, o, lo=lo, hi=hi: (jnp.clip(t - lo, 0, hi - lo - 1), 0, 0))
                for lo, hi in spans
            ],
        ),
        out_shape=[jax.ShapeDtypeStruct((hi - lo, block, total), BF16) for lo, hi in spans],
        compiler_params=pltpu.CompilerParams(vmem_limit_bytes=60 << 20),
        cost_estimate=pl.CostEstimate(
            flops=2 * rows * width * sum(r.shape[1] for r in rights), transcendentals=0,
            bytes_accessed=2 * (rows * width * len(lefts) + rows * total + width * total),
        ),
        name="owner_grad",
    )(order, *lefts, *rights)


def on_device(
    tokens,
    layer_input,
    cotangent,
    lengths,
    deal_order,
    attention_input_weight,
    attn_out,
    gate_up,
    ffn_down,
    laurel_pair,
    layer_pair,
    norm_gains,
    head_gains,
):
    sequences, positions, model_width = tokens.shape
    plane = lax.axis_index("rep")
    shard = lax.axis_index("fsdp")
    planes = lax.axis_size("rep")
    shards = lax.axis_size("fsdp")
    rows_here = sequences * positions
    window_rows = WINDOW // shards
    width_here = model_width // shards
    dims = (sequences, positions, window_rows, shards)
    over_fsdp = Exchange("fsdp", fsdp_phases(shards), shards)
    over_rep = Exchange("rep", rep_phases(planes), planes)

    spans = over_fsdp.groups()
    hidden_here = HIDDEN_UNITS // shards

    with jax.named_scope("gather_in"):
        in_w = lax.all_gather(attention_input_weight, "fsdp", axis=0, tiled=True)
    quarter = width_here // 4
    parity = plane % 2

    def by_owner(start, rows):
        parts = [
            lax.dynamic_slice(array, (start, first), (rows, HIDDEN_UNITS)).reshape(rows, shards, hidden_here)
            for array, first in ((gate_up, 0), (gate_up, HIDDEN_UNITS), (ffn_down, 0))
        ]
        return lax.optimization_barrier(jnp.concatenate([jnp.swapaxes(p, 0, 1) for p in parts], axis=2))

    with jax.named_scope("deal_part"):
        part_w = lax.all_to_all(
            by_owner((2 + parity) * quarter, quarter), "fsdp", split_axis=0, concat_axis=0, tiled=True
        )
    in_w, part_w = lax.optimization_barrier((in_w, part_w))
    with jax.named_scope("swap_part"):
        other_w = lax.ppermute(part_w, "rep", [(i, i ^ 1) for i in range(planes)])
    half_send = by_owner(0, 2 * quarter)
    small = jnp.concatenate([layer_pair, attn_out, laurel_pair], axis=1)
    gains_w = lax.all_gather(norm_gains, "fsdp", axis=1, tiled=True)
    scales = gains_w.astype(F32)
    head_scales = head_gains.astype(F32)

    count = deal_order.shape[0]
    ids = jnp.arange(count, dtype=jnp.int32)
    takes = deal_order[None, :] == ids[:, None]
    slot_of = jnp.sum(jnp.where(takes, ids[None, :], 0), axis=1)
    slot_lens = jnp.sum(jnp.where(takes, lengths[:, None], 0), axis=0)
    earlier = (ids[None, :] < ids[:, None]) & (ids[None, :] // sequences == ids[:, None] // sequences)
    slot_offsets = jnp.sum(jnp.where(earlier, slot_lens[None, :], 0), axis=1)
    offset_of = jnp.sum(jnp.where(takes, slot_offsets[None, :], 0), axis=1)
    group_of = slot_of // sequences
    home_offset = lax.dynamic_slice_in_dim(offset_of, plane * sequences, sequences)
    home_group = lax.dynamic_slice_in_dim(group_of, plane * sequences, sequences)
    home_length = lax.dynamic_slice_in_dim(lengths, plane * sequences, sequences)
    at_position = shard * positions + jnp.arange(positions, dtype=jnp.int32)
    stream = (home_offset[:, None] + at_position[None, :]).reshape(rows_here)
    live = (at_position[None, :] < home_length[:, None]).astype(F32).reshape(rows_here, 1)
    angles = stream.astype(F32)[:, None] * frequencies()[None, :]
    cosine, sine = lax.optimization_barrier((jnp.cos(angles), jnp.sin(angles)))

    far = 1 << 14
    fsdp_sources = over_fsdp.sources(shard)
    fsdp_slots = over_fsdp.slots(shard)
    plane_order = over_rep.sources(plane)
    target = (plane_order[:, None] * sequences + jnp.arange(sequences, dtype=jnp.int32)[None, :]).reshape(-1)
    picks = target[:, None] == ids[None, :]
    target_base = jnp.sum(jnp.where(picks, (group_of * far + offset_of)[None, :], 0), axis=1)
    window_at = shard * window_rows - WINDOW + jnp.arange(window_rows, dtype=jnp.int32)
    target_key = (target_base[:, None] + window_at[None, :]).reshape(-1)
    source_position = fsdp_sources[:, None] * positions + jnp.arange(positions, dtype=jnp.int32)[None, :]
    source_key = jnp.where(
        source_position[:, None, :] < home_length[None, :, None],
        (home_group * far + home_offset)[None, :, None] + source_position[:, None, :],
        -(1 << 20),
    ).reshape(-1)
    window_pick = (target_key[:, None] == source_key[None, :]).astype(BF16)

    blocks = WINDOW // positions + 1
    block_device = shard - (blocks - 1) + jnp.arange(blocks, dtype=jnp.int32)
    device_slot = jnp.sum(
        jnp.where(block_device[:, None] == jnp.arange(shards, dtype=jnp.int32)[None, :], fsdp_slots[None, :], 0),
        axis=1,
    )
    block_slot = jnp.where(block_device >= 0, device_slot, -1)
    pieces = (blocks) * (positions // window_rows)
    piece_index = jnp.clip(
        shard * (positions // window_rows) + jnp.arange(pieces, dtype=jnp.int32), 0, shards - 1
    )
    piece_slot = jnp.sum(
        jnp.where(piece_index[:, None] == jnp.arange(shards, dtype=jnp.int32)[None, :], fsdp_slots[None, :], 0),
        axis=1,
    )
    low = WINDOW - home_offset - shard * positions
    meta = jnp.concatenate([low, block_slot, piece_slot]).astype(jnp.int32)

    x_float = tokens.reshape(rows_here, model_width).astype(F32)
    layer_float = layer_input.reshape(rows_here, PER_LAYER_WIDTH).astype(F32)
    hidden = rms_norm(x_float, scales[0])
    hidden_b = to_low(hidden)
    qkv = dot(hidden_b, in_w)
    query_b, kv_b = heads_fwd(qkv, cosine, sine, head_scales, positions)
    kv_slots = jnp.concatenate(over_fsdp.pieces(kv_b.reshape(sequences, positions, 2 * KEY_WIDTH)), axis=0)
    small, half_send, kv_slots = lax.optimization_barrier((small, half_send, kv_slots))
    with jax.named_scope("deal_half"):
        half_w = lax.all_to_all(half_send, "fsdp", split_axis=0, concat_axis=0, tiled=True)
    with jax.named_scope("gather_small"):
        small_w = lax.all_gather(small, "fsdp", axis=0, tiled=True)
    out_at = 2 * PER_LAYER_WIDTH
    laurel_at = out_at + QUERY_WIDTH
    layer_w = small_w[:, :out_at]
    out_w = small_w[:, out_at:laurel_at]
    laurel_w = small_w[:, laurel_at:]
    plane_kv = kv_slots.reshape(shards * rows_here, 2 * KEY_WIDTH)
    window_part = to_low(dot(window_pick, plane_kv)).reshape(planes, sequences, window_rows, 2 * KEY_WIDTH)
    window_here = over_rep.scatter_whole(window_part)[0]
    pw_slots = jnp.concatenate(over_fsdp.pieces(window_here), axis=0)
    kv_slots = kv_slots.reshape(shards, sequences, positions, 2 * KEY_WIDTH)
    pw_slots = pw_slots.reshape(shards, sequences, window_rows, 2 * KEY_WIDTH)
    attended_b = attend_fwd(meta, query_b, kv_slots, pw_slots, dims)
    attn_proj = dot_t(attended_b, out_w)
    laurel_mid_b = to_low(dot(hidden_b, laurel_w[:, :RESIDUAL_RANK]))
    laurel_back = dot_t(laurel_mid_b, laurel_w[:, RESIDUAL_RANK:])
    first_sum = combine(x_float, attn_proj, laurel_back, hidden, scales[1], scales[2])
    ffn_in_b = to_low(rms_norm(first_sum, scales[3]))

    with jax.named_scope("join_rows"):
        ffn_w = join_rows(parity.reshape(1), half_w, part_w, other_w).reshape(model_width, 3 * hidden_here)
    cot_rows = cotangent.reshape(rows_here, model_width)
    layer_rows = layer_input.reshape(rows_here, PER_LAYER_WIDTH)
    chunks = []
    for i in range(sequences):
        rows = slice(i * positions, (i + 1) * positions)
        with jax.named_scope("gather_in_%d" % i):
            pieces = over_fsdp.pieces(ffn_in_b[rows])
        with jax.named_scope("ffn_fwd_%d" % i):
            (act_b, slope_b, value_b), ffn_in, parts = ffn_fwd(pieces, ffn_w, spans)
        ffn_w, act_b = lax.optimization_barrier((ffn_w, act_b))
        with jax.named_scope("scatter_out_%d" % i):
            mine, got = over_fsdp.scatter_pair(parts)
        with jax.named_scope("middle_%d" % i):
            outs = middle(i, positions, mine, got, first_sum, cot_rows, live, layer_rows, layer_w, scales)
        with jax.named_scope("gather_grad_%d" % i):
            grad_pieces = over_fsdp.pieces(outs[6])
        chunks.append(
            dict(
                mixed=outs[0], grad_layer_in=outs[1], second=outs[2], grad_gate_layer=outs[3], grad_back=outs[4],
                layer_mix=outs[5], grad_first=outs[7], gains=outs[8], grad_pieces=grad_pieces,
                ffn_in=ffn_in, act=act_b, slope=slope_b, value=value_b,
            )
        )
    for i, c in enumerate(chunks):
        if i == sequences - 1:
            with jax.named_scope("down_grad"):
                down_parts = rows_grad(
                    [k["grad_pieces"] for k in chunks], [[k["act"] for k in chunks]], planes, shards
                )
            ffn_w, down_parts = lax.optimization_barrier((ffn_w, down_parts))
        with jax.named_scope("ffn_bwd_%d" % i):
            c["grad_gate"], c["grad_up"], parts = ffn_bwd(c["grad_pieces"], ffn_w, c["slope"], c["value"], spans)
        ffn_w, c["grad_gate"] = lax.optimization_barrier((ffn_w, c["grad_gate"]))
        with jax.named_scope("scatter_grad_%d" % i):
            c["pair"] = over_fsdp.scatter_pair(parts)

    def joined(name):
        return jnp.concatenate([c[name] for c in chunks], axis=0)

    def listed(name):
        return [c[name] for c in chunks]

    row_part = width_here // planes

    def plane_sum(parts, name):
        with jax.named_scope("sum_" + name):
            return lax.psum_scatter(
                parts.reshape(planes * shards * row_part, parts.shape[-1]), "rep", scatter_dimension=0, tiled=True
            )

    def to_owners(mine, kinds, name):
        with jax.named_scope("deal_" + name):
            theirs = lax.all_to_all(
                mine.reshape(shards, row_part, mine.shape[-1]), "fsdp", split_axis=0, concat_axis=0, tiled=True
            )
        theirs = jnp.transpose(theirs.reshape(shards, row_part, kinds, hidden_here), (1, 2, 0, 3))
        return theirs.reshape(row_part, kinds * HIDDEN_UNITS)

    with jax.named_scope("gate_up_grad"):
        gate_up_parts = rows_grad(
            [[k["ffn_in"]] for k in chunks], [listed("grad_gate"), listed("grad_up")], planes, shards
        )
    down_sum = plane_sum(down_parts, "down")
    gate_up_sum = plane_sum(after(gate_up_parts, down_sum), "gate_up")
    with jax.named_scope("spread_down"):
        down_rows = line_gather(to_owners(down_sum, 1, "down"), "rep", planes)
    ffn_down_grad = jnp.zeros((width_here, HIDDEN_UNITS), F32)
    for r in range(planes):
        ffn_down_grad = lax.dynamic_update_slice(
            ffn_down_grad, down_rows[r].astype(F32), (((plane + r) % planes) * row_part, 0)
        )

    pairs = [c["pair"] for c in chunks]
    last = lax.optimization_barrier((pairs[-1][0], gate_up_parts))[0]
    with jax.named_scope("first_back"):
        grad_sum, grad_proj_b, grad_laurel_b, gains_back = first_back(
            [p[0] for p in pairs[:-1]] + [last], [p[1] for p in pairs], listed("grad_first"),
            first_sum, attn_proj, laurel_back, scales,
        )
    grad_mid_b = to_low(dot(grad_laurel_b, laurel_w[:, RESIDUAL_RANK:]))
    grad_attended_b = to_low(dot(grad_proj_b, out_w))
    with jax.named_scope("small_grad"):
        joined_mid = jnp.concatenate([grad_mid_b, jnp.zeros_like(grad_mid_b)], axis=1)
        mid_joined = jnp.concatenate([jnp.zeros_like(laurel_mid_b), laurel_mid_b], axis=1)
        small_parts = owner_grad(
            fsdp_sources,
            [joined("second"), joined("grad_back"), grad_proj_b, hidden_b, grad_laurel_b],
            [joined("grad_gate_layer"), joined("layer_mix"), attended_b, joined_mid, mid_joined],
            [False, False, False, False, True],
            spans,
        )
    with jax.named_scope("attend_bwd"):
        grad_query, gkv_part, gpw_part = attend_bwd(meta, query_b, kv_slots, pw_slots, grad_attended_b, dims)
    grad_q_b, grad_q_head = heads_bwd(
        qkv, 0, QUERY_HEADS, QUERY_HEADS, cosine, sine, head_scales[0:1], grad_query, positions
    )
    with jax.named_scope("query_grad"):
        query_parts = owner_grad(fsdp_sources, [hidden_b], [grad_q_b], [False], spans)
    with jax.named_scope("window_back"):
        gpw_here = over_fsdp.scatter_whole(gpw_part.reshape(shards * sequences, window_rows, 2 * KEY_WIDTH))
        gpw_all = jnp.concatenate(over_rep.pieces(gpw_here), axis=0).reshape(-1, 2 * KEY_WIDTH)
    gkv_sum = t_dot(window_pick, gpw_all) + gkv_part.reshape(-1, 2 * KEY_WIDTH).astype(F32)
    with jax.named_scope("keys_back"):
        grad_kv = over_fsdp.scatter_whole(
            to_low(gkv_sum).reshape(shards * sequences, positions, 2 * KEY_WIDTH)
        ).reshape(rows_here, 2 * KEY_WIDTH)
    grad_kv_b, grad_k_head = heads_bwd(
        qkv, QUERY_HEADS, 2 * KEY_VALUE_HEADS, KEY_VALUE_HEADS, cosine, sine, head_scales[1:2], grad_kv, positions
    )
    with jax.named_scope("keys_grad"):
        keys_parts = owner_grad(fsdp_sources, [hidden_b], [grad_kv_b], [False], spans)
    grad_hidden = (
        grad_sum
        + dot_t(grad_mid_b, laurel_w[:, :RESIDUAL_RANK])
        + dot_t(grad_q_b, in_w[:, :QUERY_WIDTH])
        + dot_t(grad_kv_b, in_w[:, QUERY_WIDTH:])
    )
    unused_norm, pull_in = jax.vjp(rms_norm, x_float, scales[0])
    grad_x_two, gain_zero = pull_in(grad_hidden)
    input_grad = to_low(grad_sum + grad_x_two).reshape(tokens.shape)

    def owned(parts, name):
        with jax.named_scope("own_" + name):
            return over_fsdp.scatter(parts)[0]

    early = jnp.concatenate([owned(small_parts, "small"), owned(query_parts, "query")], axis=1)
    with jax.named_scope("all_early"):
        early = lax.psum(after(early, gate_up_sum), "rep")
    gate_up_rows = to_owners(gate_up_sum, 2, "gate_up")
    with jax.named_scope("spread_gate_up"):
        gate_up_grad = lax.all_gather(after(gate_up_rows, early), "rep", axis=0, tiled=True)
    keys_grad = owned(keys_parts, "keys")
    with jax.named_scope("all_keys"):
        keys_grad = lax.psum(after(keys_grad, gate_up_grad), "rep")
    gate_up_grad = gate_up_grad.astype(F32)
    early = early.astype(F32)
    small_width = laurel_at + 2 * RESIDUAL_RANK
    attn_in_grad = jnp.concatenate([early[:, small_width:], keys_grad.astype(F32)], axis=1)

    gain_rows = jnp.concatenate([gain_zero[None], gains_back, sum(c["gains"] for c in chunks)], axis=0)
    grad_head = jnp.concatenate([grad_q_head, grad_k_head], axis=0)
    packed = jnp.concatenate([gain_rows, jnp.pad(grad_head, ((0, 0), (0, model_width - HEAD_DIM)))], axis=0)
    packed = over_rep.total(over_fsdp.total(packed))
    gain_share = lax.dynamic_slice_in_dim(packed[:6], shard * width_here, width_here, 1)
    return (
        jnp.stack([c["mixed"] for c in chunks]),
        input_grad,
        jnp.stack([c["grad_layer_in"] for c in chunks]),
        attn_in_grad,
        early[:, out_at:laurel_at],
        gate_up_grad,
        ffn_down_grad,
        early[:, laurel_at:small_width],
        early[:, :out_at],
        gain_share,
        packed[6:8, :HEAD_DIM],
    )


def solution(mesh):
    rows = P("rep", "fsdp", None)
    weight = P("fsdp", None)
    return jax.shard_map(
        on_device,
        mesh=mesh,
        in_specs=(rows, rows, rows, P(), P()) + (weight,) * 6 + (P(None, "fsdp"), P()),
        out_specs=(rows, rows, rows) + (weight,) * 6 + (P(None, "fsdp"), P()),
        check_vma=False,
    )
```
